128 devices in a mesh: db: 8 (over z, x_lo), tp: 16 (over y, x_hi, core).
Axes of the slice: x: 4 (x_hi: 2, x_lo: 2; x = x_hi * 2 + x_lo), y: 4, z: 4, core: 2. Of those that a mesh axis runs over, the one named last changes fastest.
Arguments:
- queries: bfloat16 [32768, 1024], P('db', 'tp'), may hold values from -6 to 6
- enc_up: bfloat16 [1024, 4096], P(None, 'tp'), may hold values from -0.1875 to 0.1875
- enc_down: bfloat16 [4096, 1024], P('tp'), may hold values from -0.09375 to 0.09375
- attn_gain: float32 [1024], replicated, may hold values from 0.25 to 1.75
- w_query: bfloat16 [1024, 1024], P(None, 'tp'), may hold values from -0.1875 to 0.1875
- w_keyval: bfloat16 [2, 1024, 1024], replicated, may hold values from -0.1875 to 0.1875
- w_out: bfloat16 [1024, 1024], P('tp'), may hold values from -0.1875 to 0.1875
- database: float32 [2048, 128, 1024], P('db', 'tp'), may hold values from -6 to 6
- nb_owner: int32 [512, 2], P('db'), may hold values from 0 to 7, as said below
- nb_row: int32 [512, 2], P('db'), may hold values from 0 to 255
Outputs:
- mixed: bfloat16 [32768, 1024], P('db', 'tp')
The draws below stay inside these ranges and needn't reach their ends.
Inputs may be any that keep to these rules, and one draw needn't show every extreme that they name: `nb_owner`: among the neighbour ids of one db index's 64 stretches, no owner is named more than 32 times, and some owner is named exactly 32 times.
All inputs are finite; a program needn't handle non-finite values.
Results may differ from the reference program's by a relative error of at most 0.02.
Values may be sent and summed in bfloat16 or wider, within the bound.
A program may use at most 128 MiB of HBM per device.

```python
import jax
import jax.numpy as jnp
from jax import lax

D = 1024
FF = 4096
HEADS = 16
HEAD_DIM = 64
STRETCH = 64
NB_LEN = 128
K_NB = 2
CH_DB = 64
BLK_DEV = 256
CAP = 32
STRETCHES = 512
TOKENS = 32768
BLOCKS = 2048
N_DB = 8
N_TP = 16


def draw_nb_owner(key, part):
    per_group = CH_DB * K_NB

    def one_group(group_key):
        key_hot, key_order, key_place = jax.random.split(group_key, 3)
        hot = jax.random.randint(key_hot, (), 0, N_DB)
        slot_owner = jnp.arange(N_DB * CAP, dtype=jnp.int32) // CAP
        noise = jax.random.permutation(key_order, N_DB * CAP).astype(jnp.int32)
        score = jnp.where(slot_owner == hot, -1, noise)
        order = jnp.argsort(score, stable=True)
        chosen = slot_owner[order[:per_group]]
        return jax.random.permutation(key_place, chosen)
    group_keys = jax.random.split(jax.random.fold_in(key, 17), N_DB)
    owners = jax.vmap(one_group)(group_keys)
    return owners.reshape(STRETCHES, K_NB).astype(jnp.int32)


def place_ends(values, rng, least, high):
    place = [jax.random.randint(jax.random.fold_in(rng, axis), (), 0, length) for axis, length in enumerate(values.shape)]
    widest = values.shape.index(max(values.shape))
    neighbour = place[:widest] + [(place[widest] + 1) % values.shape[widest]] + place[widest + 1:]
    return values.at[tuple(place)].set(least).at[tuple(neighbour)].set(high)


def level_of(own_key, dims, cuts, smallest, largest):
    level = 1.0
    for position, blocks in cuts:
        heights = jax.random.uniform(jax.random.fold_in(jax.random.fold_in(own_key, 6), position), (blocks,), jnp.float32, smallest / len(cuts), largest / len(cuts))
        level = level * jnp.repeat(jnp.exp(heights), dims[position] // blocks).reshape((-1,) + (1,) * (len(dims) - 1 - position))
    return level


def centred(stream_key, shape, spread, most, cuts=(), kind=jnp.bfloat16):
    factor_of = level_of(stream_key, shape, cuts, -0.22, 0.18) if cuts else 1.0
    entries = jax.random.normal(stream_key, shape, jnp.float32) * spread * factor_of
    return jnp.minimum(jnp.maximum(entries, -most), most).astype(kind)


def setup_inputs(seed: int = 0) -> dict:
    key_list = jax.random.split(jax.random.key(seed), 11)
    queries = centred(key_list[0], (TOKENS, D), 1.0, 6.0, ((0, 8), (1, 16)))
    enc_up = centred(key_list[1], (D, FF), D ** -0.5, 0.1875, ((1, 16),))
    enc_down = centred(key_list[2], (FF, D), FF ** -0.5, 0.09375, ((0, 16),))
    attn_gain = jnp.clip(1.0 + 0.15 * jax.random.normal(key_list[3], (D,), jnp.float32), 0.25, 1.75)
    w_query = centred(key_list[4], (D, D), D ** -0.5, 0.1875, ((1, 16),))
    w_keyval = centred(key_list[5], (2, D, D), D ** -0.5, 0.1875)
    w_out = centred(key_list[6], (D, D), D ** -0.5, 0.1875, ((0, 16),))
    database = centred(key_list[7], (BLOCKS, NB_LEN, D), 1.0, 6.0, ((0, 8), (1, 16)), jnp.float32)
    nb_owner = draw_nb_owner(jax.random.fold_in(key_list[10], 71), 0)
    nb_row = place_ends(jax.random.randint(key_list[9], (STRETCHES, K_NB), 0, BLK_DEV), jax.random.fold_in(key_list[9], 1), 0, BLK_DEV - 1).astype(jnp.int32)
    return {"queries": queries, "enc_up": enc_up, "enc_down": enc_down, "attn_gain": attn_gain, "w_query": w_query, "w_keyval": w_keyval, "w_out": w_out, "database": database, "nb_owner": nb_owner, "nb_row": nb_row}


def rounded_terms(left, right, width, count):
    total = jnp.zeros((left.shape[0], right.shape[1]), jnp.float32)
    for index in range(count):
        term = jnp.dot(left[:, index * width:(index + 1) * width], right[index * width:(index + 1) * width], preferred_element_type=jnp.float32)
        term = lax.optimization_barrier(term.astype(jnp.bfloat16))
        total = total + term.astype(jnp.float32)
    return total

def reference(queries, enc_up, enc_down, attn_gain, w_query, w_keyval, w_out, database, nb_owner, nb_row):
    hidden = jax.nn.gelu(jnp.dot(queries, enc_up, preferred_element_type=jnp.float32), approximate=True).astype(jnp.bfloat16)
    summed = rounded_terms(hidden, enc_down, FF // N_TP, N_TP)
    encoded = (queries.astype(jnp.float32) + summed).astype(jnp.bfloat16)
    enc_float = encoded.astype(jnp.float32)
    scale_row = lax.rsqrt(lax.optimization_barrier(jnp.mean(enc_float * enc_float, axis=1, keepdims=True)) + 1e-06)
    normed = (enc_float * scale_row * attn_gain[None, :]).astype(jnp.bfloat16)
    query_heads = jnp.dot(normed, w_query, preferred_element_type=jnp.float32).astype(jnp.bfloat16)
    flat_ids = (nb_owner * BLK_DEV + nb_row).astype(jnp.int32)
    scale = HEAD_DIM ** (-0.5)

    def per_stretch(inputs):
        ids, block_q = inputs
        near = database[ids].reshape(K_NB * NB_LEN, D).astype(jnp.bfloat16)
        keys = jnp.dot(near, w_keyval[0], preferred_element_type=jnp.float32).astype(jnp.bfloat16)
        values = jnp.dot(near, w_keyval[1], preferred_element_type=jnp.float32).astype(jnp.bfloat16)
        keys = keys.reshape(K_NB * NB_LEN, HEADS, HEAD_DIM).astype(jnp.float32)
        values = values.reshape(K_NB * NB_LEN, HEADS, HEAD_DIM).astype(jnp.float32)
        heads_q = block_q.reshape(STRETCH, HEADS, HEAD_DIM).astype(jnp.float32)
        scores = jnp.einsum('qhd,khd->hqk', heads_q, keys) * scale
        weights = jax.nn.softmax(scores, axis=-1).astype(jnp.bfloat16)
        context = jnp.einsum('hqk,khd->qhd', weights.astype(jnp.float32), values).astype(jnp.bfloat16)
        return context.reshape(STRETCH, D)
    context = lax.map(per_stretch, (flat_ids, query_heads.reshape(STRETCHES, STRETCH, D)))
    context = context.reshape(TOKENS, D)
    projected = rounded_terms(context, w_out, D // N_TP, N_TP)
    return (enc_float + projected).astype(jnp.bfloat16)
```

```python
import jax
import jax.numpy as jnp
from jax import lax
from jax.experimental import pallas as pl
from jax.experimental.pallas import tpu as pltpu
from jax.sharding import PartitionSpec as P

MESH = pl.DeviceIdType.MESH
BF = jnp.bfloat16
F32 = jnp.float32
ANY = pl.BlockSpec(memory_space=pl.ANY)
VM = pl.BlockSpec(memory_space=pltpu.VMEM)
SM = pl.BlockSpec(memory_space=pltpu.SMEM)


def place():
    d = lax.axis_index("db")
    t = lax.axis_index("tp")
    return d, t, d % 2, t // 4, (t // 2) % 2, t % 2


def greet(peers):
    sem = pltpu.get_barrier_semaphore()
    for peer in peers:
        pl.semaphore_signal(sem, inc=1, device_id=peer, device_id_type=MESH)
    pl.semaphore_wait(sem, len(peers))


def remote(src, dst, send, recv, dev):
    return pltpu.make_async_remote_copy(
        src_ref=src, dst_ref=dst, send_sem=send, recv_sem=recv, device_id=dev, device_id_type=MESH
    )


def in_kernel(
    slot, want, qt, up, down, wqt, wo, base,
    xbuf, upall, downall, wqall, woall, near,
    basev, sbuf, rbuf, pbuf, asked, asked_s,
    base_sem, ask_s, ask_r, ask_l, q_s, q_r, q_l, w_s, w_r, w_l, f_s, f_r, h_s, h_r, hf_s, hf_r,
    a_s, a_r, b_s, b_r, b_l,
):
    d, t, xlo, y, xhi, c = place()
    sib = t + 1 - 2 * c
    load = pltpu.make_async_copy(base, basev, base_sem)
    load.start()
    db_peers = [lax.rem(d + k, 8) for k in (4, 5, 3, 2, 6, 7, 1)]
    tp_peers = [lax.rem(t + k, 16) for k in range(1, 16)]
    y_peers = [lax.rem(t + 4 * k, 16) for k in (1, 3, 2)]
    across = (d + 1 - 2 * xlo, t + 2 - 4 * xhi)
    greet([(g, t) for g in db_peers] + [(d, s) for s in tp_peers] + [across])

    waits = []
    asks = []
    for i, g in enumerate(db_peers):
        cp = remote(want.at[g], asked.at[d], ask_s.at[i], ask_r.at[d], (g, t))
        cp.start()
        asks.append((cp, g))
    own_ask = pltpu.make_async_copy(want.at[d], asked.at[d], ask_l.at[0])
    own_ask.start()

    mine = 2 * y + c
    for i, s in enumerate(y_peers):
        for j, (src, dst, at) in enumerate(
            ((up, upall, mine), (down, downall, mine), (wqt, wqall, t), (wo, woall, t))
        ):
            cp = remote(src, dst.at[at], w_s.at[4 * i + j], w_r.at[4 * y + j], (d, s))
            cp.start()
            waits.append(cp.wait_send)
    own = []
    for j, (src, dst, at) in enumerate(
        ((up, upall, mine), (down, downall, mine), (wqt, wqall, t), (wo, woall, t))
    ):
        cp = pltpu.make_async_copy(src, dst.at[at], w_l.at[j])
        cp.start()
        own.append(cp)
        cp = remote(src, dst.at[at], f_s.at[4 * y + j], f_r.at[4 * y + j], (d, sib))
        cp.start()
        waits.append(cp.wait_send)

    for i, s in enumerate(tp_peers):
        to = (s // 4) * 4 + s % 2
        for p in range(2):
            col = pl.multiple_of(256 * (to + 2 * p), 256)
            cp = remote(
                qt.at[:, pl.ds(col, 256)],
                xbuf.at[p, pl.ds(pl.multiple_of(64 * t, 64), 64), :],
                q_s.at[2 * i + p], q_r.at[2 * t + p], (d, s),
            )
            cp.start()
            waits.append(cp.wait_send)
    for p in range(2):
        col = pl.multiple_of(256 * (4 * y + c + 2 * p), 256)
        cp = pltpu.make_async_copy(
            qt.at[:, pl.ds(col, 256)],
            xbuf.at[p, pl.ds(pl.multiple_of(64 * t, 64), 64), :], q_l.at[p])
        cp.start()
        own.append(cp)

    own_ask.wait()
    for cp, g in asks:
        cp.wait_send()
        remote(want.at[d], asked.at[g], ask_s.at[0], ask_r.at[g], (g, t)).wait_recv()
    to_s = pltpu.make_async_copy(asked, asked_s, ask_l.at[1])
    to_s.start()
    to_s.wait()
    load.wait()

    def pack(g, dst, at):
        def body(r, carry):
            dst[at, r] = basev[asked_s[g, 0, r]].astype(BF)
            return carry
        lax.fori_loop(0, 32, body, 0, unroll=4)

    for i, g in enumerate(db_peers):
        pack(g, sbuf, g)
        cp = remote(sbuf.at[g], rbuf.at[d], a_s.at[i], a_r.at[d], (g, t))
        cp.start()
        waits.append(cp.wait_send)
    pack(d, rbuf, d)

    for cp in own:
        cp.wait()
    across_waits = []
    for j, (src, dst) in enumerate(((wqt, wqall), (wo, woall))):
        cp = remote(src, dst.at[t], h_s.at[2 * y + j], h_r.at[2 * y + j], across)
        cp.start()
        waits.append(cp.wait_send)
    for i, s in enumerate(y_peers):
        ys = s // 4
        for j, (src, dst, at) in enumerate(
            ((up, upall, 2 * ys + c), (down, downall, 2 * ys + c), (wqt, wqall, s), (wo, woall, s))
        ):
            remote(src, dst.at[at], w_s.at[0], w_r.at[4 * ys + j], (d, s)).wait_recv()
            cp = remote(dst.at[at], dst.at[at], f_s.at[4 * ys + j], f_r.at[4 * ys + j], (d, sib))
            cp.start()
            waits.append(cp.wait_send)
            if j >= 2:
                cp = remote(dst.at[at], dst.at[at], h_s.at[2 * ys + j - 2], h_r.at[2 * ys + j - 2], across)
                cp.start()
                waits.append(cp.wait_send)
    for ys in range(4):
        for j, (src, dst) in enumerate(((wqt, wqall), (wo, woall))):
            at = 4 * ys + 2 * (1 - xhi) + c
            remote(src, dst.at[at], h_s.at[0], h_r.at[2 * ys + j], across).wait_recv()
            cp = remote(dst.at[at], dst.at[at], hf_s.at[2 * ys + j], hf_r.at[2 * ys + j], (d, sib))
            cp.start()
            waits.append(cp.wait_send)

    for i, g in enumerate(db_peers):
        remote(sbuf.at[g], rbuf.at[g], a_s.at[0], a_r.at[g], (g, t)).wait_recv()
    for i, s in enumerate(tp_peers):
        for b in range(8):
            k = slot[s * 8 + b]
            pbuf[s, b] = rbuf[k // 32, k % 32]
        cp = remote(pbuf.at[s], near.at[:, t], b_s.at[i], b_r.at[t], (d, s))
        cp.start()
        waits.append(cp.wait_send)
    for b in range(8):
        k = slot[t * 8 + b]
        pbuf[t, b] = rbuf[k // 32, k % 32]
    last = pltpu.make_async_copy(pbuf.at[t], near.at[:, t], b_l.at[0])
    last.start()

    for s in tp_peers:
        for p in range(2):
            remote(
                qt.at[:, pl.ds(0, 256)], xbuf.at[p, pl.ds(pl.multiple_of(64 * s, 64), 64), :],
                q_s.at[0], q_r.at[2 * s + p], (d, s)).wait_recv()
        remote(pbuf.at[s], near.at[:, s], b_s.at[0], b_r.at[s], (d, s)).wait_recv()
    for ys in range(4):
        for j, (src, dst, at) in enumerate(
            ((up, upall, 2 * ys + 1 - c), (down, downall, 2 * ys + 1 - c),
             (wqt, wqall, 4 * ys + 2 * xhi + 1 - c), (wo, woall, 4 * ys + 2 * xhi + 1 - c))
        ):
            remote(src, dst.at[at], f_s.at[0], f_r.at[4 * ys + j], (d, sib)).wait_recv()
        for j, (src, dst) in enumerate(((wqt, wqall), (wo, woall))):
            at = 4 * ys + 2 * (1 - xhi) + 1 - c
            remote(src, dst.at[at], hf_s.at[0], hf_r.at[2 * ys + j], (d, sib)).wait_recv()
    last.wait()
    for w in waits:
        w()


def fetch(slot, want, qt, up, down, wqt, wo, base):
    D = pltpu.SemaphoreType.DMA
    return pl.pallas_call(
        in_kernel,
        name="fetch",
        out_shape=(
            jax.ShapeDtypeStruct((2, 1024, 256), BF),
            jax.ShapeDtypeStruct((8, 1024, 256), BF),
            jax.ShapeDtypeStruct((8, 256, 1024), BF),
            jax.ShapeDtypeStruct((16, 64, 1024), BF),
            jax.ShapeDtypeStruct((16, 64, 1024), BF),
            jax.ShapeDtypeStruct((8, 16, 8, 1024), BF),
        ),
        in_specs=[SM, VM, ANY, ANY, ANY, ANY, ANY, ANY],
        out_specs=(ANY,) * 6,
        scratch_shapes=[
            pltpu.VMEM((256, 8, 1024), F32),
            pltpu.VMEM((8, 32, 8, 1024), BF),
            pltpu.VMEM((8, 32, 8, 1024), BF),
            pltpu.VMEM((16, 8, 8, 1024), BF),
            pltpu.VMEM((8, 8, 128), jnp.int32),
            pltpu.SMEM((8, 8, 128), jnp.int32),
            D, D((7,)), D((8,)), D((2,)), D((30,)), D((32,)), D((2,)),
            D((12,)), D((16,)), D((4,)), D((16,)), D((16,)),
            D((8,)), D((8,)), D((8,)), D((8,)),
            D((7,)), D((8,)), D((15,)), D((16,)), D((1,)),
        ],
        compiler_params=pltpu.CompilerParams(
            collective_id=0, has_side_effects=True, vmem_limit_bytes=56 << 20
        ),
    )(slot, want, qt, up, down, wqt, wo, base)


def swap_kernel(part, out, s, r):
    d, t, xlo, y, xhi, c = place()
    other = (d, t + 2 - 4 * xhi)
    greet([other])
    cp = remote(part.at[1 - xhi], out, s, r, other)
    cp.start()
    cp.wait()


def swap(part):
    return pl.pallas_call(
        swap_kernel,
        name="swap",
        out_shape=jax.ShapeDtypeStruct((256, 1024), BF),
        in_specs=[ANY],
        out_specs=ANY,
        scratch_shapes=[pltpu.SemaphoreType.DMA, pltpu.SemaphoreType.DMA],
        compiler_params=pltpu.CompilerParams(collective_id=1, has_side_effects=True),
    )(part)


def out_kernel(mixed, out, send, recv, own):
    d, t, xlo, y, xhi, c = place()
    peers = [lax.rem(t + k, 16) for k in range(1, 16)]
    greet([(d, s) for s in peers])
    col = pl.ds(pl.multiple_of(256 * t, 256), 256)
    cps = []
    for i, s in enumerate(peers):
        cp = remote(mixed.at[s], out.at[:, col], send.at[i], recv.at[t], (d, s))
        cp.start()
        cps.append(cp)
    lc = pltpu.make_async_copy(mixed.at[t], out.at[:, col], own)
    lc.start()
    for i, s in enumerate(peers):
        cps[i].wait_send()
        remote(
            mixed.at[s], out.at[:, pl.ds(pl.multiple_of(256 * s, 256), 256)],
            send.at[0], recv.at[s], (d, s)).wait_recv()
    lc.wait()


def give(mixed):
    D = pltpu.SemaphoreType.DMA
    return pl.pallas_call(
        out_kernel,
        name="give",
        out_shape=jax.ShapeDtypeStruct((64, 4096), BF),
        in_specs=[ANY],
        out_specs=ANY,
        scratch_shapes=[D((15,)), D((16,)), D],
        compiler_params=pltpu.CompilerParams(collective_id=2, has_side_effects=True),
    )(mixed)


def per_device(
    queries, enc_up, enc_down, attn_gain, w_query, w_keyval, w_out, database, nb_owner, nb_row
):
    owners = nb_owner.reshape(128)
    rows = nb_row.reshape(128)
    i = jnp.arange(128)
    rank = jnp.sum(
        ((owners[:, None] == owners[None, :]) & (i[None, :] < i[:, None])).astype(jnp.int32), axis=1)
    slot = owners * 32 + rank
    lane = jnp.arange(128)
    key = jnp.where(lane < 32, lane, -1)[None, :] + 32 * jnp.arange(8)[:, None]
    key = jnp.where((lane < 32)[None, :], key, -1)
    want = jnp.sum(
        jnp.where(key[:, :, None] == slot[None, None, :], rows[None, None, :], 0), axis=2)
    want = jnp.broadcast_to(want[:, None, :], (8, 8, 128))
    x, up, down, wq, wo, near = fetch(
        slot, want, queries.T, enc_up, enc_down, w_query.T, w_out, database)
    xhi = (lax.axis_index("tp") // 2) % 2
    hidden = jax.nn.gelu(
        jnp.einsum("pft,kfh->ptkh", x, up, preferred_element_type=F32), approximate=True).astype(BF)
    part = jnp.einsum("ptkh,khd->ptd", hidden, down, preferred_element_type=F32)
    other = swap(part.astype(BF))
    part_own = lax.dynamic_index_in_dim(part, xhi, 0, keepdims=False)
    x_own = lax.dynamic_index_in_dim(x, xhi, 0, keepdims=False).T
    encoded = (x_own.astype(F32) + (part_own + other.astype(F32))).astype(BF)
    ef = encoded.astype(F32)
    scale = lax.rsqrt(jnp.mean(ef * ef, axis=1, keepdims=True) + 1e-06)
    normed = (ef * scale * attn_gain[None, :]).astype(BF)
    q = jnp.einsum("td,ed->te", normed, wq.reshape(1024, 1024), preferred_element_type=F32).astype(BF)
    kv = jnp.einsum("td,sde->ste", near.reshape(1024, 1024), w_keyval, preferred_element_type=F32).astype(BF)
    k = kv[0].reshape(4, 256, 16, 64)
    v = kv[1].reshape(4, 256, 16, 64)
    qh = q.reshape(4, 64, 16, 64)
    scores = jnp.einsum("cqhd,ckhd->chqk", qh, k, preferred_element_type=F32) * 0.125
    w = jax.nn.softmax(scores, axis=-1).astype(BF)
    ctx = jnp.einsum("chqk,ckhd->cqhd", w, v, preferred_element_type=F32).astype(BF).reshape(256, 1024)
    out = jnp.dot(ctx, wo.reshape(1024, 1024), preferred_element_type=F32)
    mixed = (ef + out).astype(BF)
    return give(mixed.T.reshape(16, 64, 256)).T


def solution(mesh):
    placed = (
        P("db", "tp"),
        P(None, "tp"),
        P("tp", None),
        P(),
        P(None, "tp"),
        P(),
        P("tp", None),
        P("db", "tp", None),
        P("db", None),
        P("db", None),
    )
    return jax.shard_map(
        per_device, mesh=mesh, in_specs=placed, out_specs=P("db", "tp"), check_vma=False
    )
```

```python
import jax
import jax.numpy as jnp
from jax import lax
from jax.experimental import pallas as pl
from jax.experimental.pallas import tpu as pltpu
from jax.sharding import PartitionSpec as P

MESH = pl.DeviceIdType.MESH
BF = jnp.bfloat16
F32 = jnp.float32
ANY = pl.BlockSpec(memory_space=pl.ANY)
VM = pl.BlockSpec(memory_space=pltpu.VMEM)
SM = pl.BlockSpec(memory_space=pltpu.SMEM)
CHUNKS = 4
WIDE = 1024 // CHUNKS


def remote(src, dst, send, recv, dev):
    return pltpu.make_async_remote_copy(
        src_ref=src, dst_ref=dst, send_sem=send, recv_sem=recv, device_id=dev, device_id_type=MESH
    )


def dot(a, b, dims):
    return lax.dot_general(a, b, (dims, ((), ())), preferred_element_type=F32)


def step_kernel(
    slot, want, gain, qt, up, down, wqt, wo, wkv, base,
    out,
    basev, sbuf, rbuf0, rbuf1, rbuf2, rbuf3, pbuf, near, xbuf, xtok, upall, downall, wqall, woall, wkvv,
    part, psend, precv, encoded, query, acc, ctx, outt, asked, asked_s,
    base_sem, ask_s, ask_r, ask_l, q_s, q_r, q_l, w_s, w_r, w_l, f_s, f_r, h_s, h_r, hf_s, hf_r,
    a_s, a_r, b_s, b_r, b_l, p_s, p_r, g_s, g_r, g_l,
):
    rbuf = (rbuf0, rbuf1, rbuf2, rbuf3)
    d = lax.axis_index("db")
    t = lax.axis_index("tp")
    xlo, y, xhi, c = d % 2, t // 4, (t // 2) % 2, t % 2
    sib = t + 1 - 2 * c
    flip = t + 2 - 4 * xhi
    load = pltpu.make_async_copy(base, basev, base_sem)
    load.start()
    near_peers = [lax.rem(d + k, 8) for k in (4, 2, 6)]
    lo_peers = [lax.rem(d + k, 8) + 1 - 2 * xlo for k in (4, 2, 6, 0)]
    db_peers = near_peers + lo_peers
    tp_peers = [lax.rem(t + k, 16) for k in range(1, 16)]
    y_peers = [lax.rem(t + 4 * k, 16) for k in (1, 3, 2)]
    across = (d + 1 - 2 * xlo, flip)

    sem = pltpu.get_barrier_semaphore()
    greeted = [(g, t) for g in db_peers] + [(d, s) for s in tp_peers] + [(g, flip) for g in lo_peers]
    for peer in greeted:
        pl.semaphore_signal(sem, inc=1, device_id=peer, device_id_type=MESH)
    pl.semaphore_wait(sem, len(greeted))

    waits = []
    asks = []
    for i, g in enumerate(db_peers):
        cp = remote(want.at[g], asked.at[d], ask_s.at[i], ask_r.at[d], (g, t))
        cp.start()
        asks.append((cp, g))
    own_ask = pltpu.make_async_copy(want.at[d], asked.at[d], ask_l.at[0])
    own_ask.start()

    mine = 2 * y + c
    weights = lambda ys, core: (
        (wqt, wqall, 4 * ys + 2 * xhi + core), (wo, woall, 4 * ys + 2 * xhi + core),
        (up, upall, 2 * ys + core), (down, downall, 2 * ys + core))
    for j, (src, dst, at) in enumerate(weights(y, c)):
        for i, s in enumerate(y_peers):
            cp = remote(src, dst.at[at], w_s.at[4 * i + j], w_r.at[4 * y + j], (d, s))
            cp.start()
            waits.append(cp.wait_send)
    own = []
    for j, (src, dst, at) in enumerate(weights(y, c)):
        cp = pltpu.make_async_copy(src, dst.at[at], w_l.at[j])
        cp.start()
        own.append(cp)
        cp = remote(src, dst.at[at], f_s.at[4 * y + j], f_r.at[4 * y + j], (d, sib))
        cp.start()
        waits.append(cp.wait_send)
        if j < 2:
            cp = remote(src, dst.at[at], h_s.at[2 * y + j], h_r.at[2 * y + j], across)
            cp.start()
            waits.append(cp.wait_send)

    feat = lambda s: pl.ds(pl.multiple_of(64 * s, 64), 64)
    for i, s in enumerate(tp_peers):
        to = (s // 4) * 4 + s % 2
        for p in range(2):
            col = pl.multiple_of(256 * (to + 2 * p), 256)
            cp = remote(
                qt.at[:, pl.ds(col, 256)], xbuf.at[p, feat(t), :],
                q_s.at[2 * i + p], q_r.at[2 * t + p], (d, s))
            cp.start()
            waits.append(cp.wait_send)
    for p in range(2):
        col = pl.multiple_of(256 * (4 * y + c + 2 * p), 256)
        cp = pltpu.make_async_copy(
            qt.at[:, pl.ds(col, 256)], xbuf.at[p, feat(t), :], q_l.at[p])
        cp.start()
        own.append(cp)
    cp = pltpu.make_async_copy(wkv, wkvv, w_l.at[4])
    cp.start()
    own.append(cp)

    own_ask.wait()
    for cp, g in asks:
        cp.wait_send()
        remote(want.at[d], asked.at[g], ask_s.at[0], ask_r.at[g], (g, t)).wait_recv()
    to_s = pltpu.make_async_copy(asked, asked_s, ask_l.at[1])
    to_s.start()
    to_s.wait()
    load.wait()

    def pack(f, g, dst):
        def body(r, carry):
            dst[f, g, r] = basev[asked_s[g, 0, r], :, WIDE * f:WIDE * (f + 1)].astype(BF)
            return carry
        lax.fori_loop(0, 32, body, 0, unroll=8)

    def pack_own(f):
        def body(r, carry):
            rbuf[f][d, r] = basev[asked_s[d, 0, r], :, WIDE * f:WIDE * (f + 1)].astype(BF)
            return carry
        lax.fori_loop(0, 32, body, 0, unroll=8)

    def first_pieces(f):
        pieces = [(pl.ds(0, 32), g, t, 0) for g in near_peers]
        for g in lo_peers:
            pieces += [(pl.ds(0, 16), g, t, 0), (pl.ds(16, 16), g, flip, 1)]
        return pieces

    for f in range(CHUNKS):
        n = 0
        for k, g in enumerate(db_peers):
            pack(f, g, sbuf)
            for rows, to, at, half in first_pieces(f):
                if to is g:
                    cp = remote(
                        sbuf.at[f, g, rows], rbuf[f].at[d, rows],
                        a_s.at[11 * f + n], a_r.at[16 * f + 2 * d + half], (g, at))
                    cp.start()
                    waits.append(cp.wait_send)
                    n += 1
        pack_own(f)

    for cp in own:
        cp.wait()
    for s in tp_peers:
        for p in range(2):
            remote(
                qt.at[:, pl.ds(0, 256)], xbuf.at[p, feat(s), :],
                q_s.at[0], q_r.at[2 * s + p], (d, s)).wait_recv()
    for p in range(2):
        xtok[p] = xbuf[p].astype(F32).T.astype(BF)

    def feed(at, first):
        def body(p, carry):
            h = dot(xtok[p], upall[at], ((1,), (0,)))
            h = jax.nn.gelu(h, approximate=True).astype(BF)
            term = dot(h, downall[at], ((1,), (0,)))
            if first:
                part[p] = term
            else:
                part[p] += term
            return carry
        lax.fori_loop(0, 2, body, 0)

    def from_sibling(ys, js):
        for j, (src, dst, at) in enumerate(weights(ys, 1 - c)):
            if j in js:
                remote(src, dst.at[at], f_s.at[0], f_r.at[4 * ys + j], (d, sib)).wait_recv()

    def from_y(s, js):
        ys = s // 4
        for j, (src, dst, at) in enumerate(weights(ys, c)):
            if j not in js:
                continue
            remote(src, dst.at[at], w_s.at[0], w_r.at[4 * ys + j], (d, s)).wait_recv()
            cp = remote(dst.at[at], dst.at[at], f_s.at[4 * ys + j], f_r.at[4 * ys + j], (d, sib))
            cp.start()
            waits.append(cp.wait_send)
            if j < 2:
                cp = remote(dst.at[at], dst.at[at], h_s.at[2 * ys + j], h_r.at[2 * ys + j], across)
                cp.start()
                waits.append(cp.wait_send)

    def second(f):
        for rows, g, at, half in first_pieces(f):
            remote(
                sbuf.at[f, g, rows], rbuf[f].at[g, rows],
                a_s.at[0], a_r.at[16 * f + 2 * g + half], (g, at)).wait_recv()
        for i, s in enumerate(tp_peers + [t]):
            for b in range(8):
                k = slot[s * 8 + b]
                pbuf[f, s, b // 2, 8 * (b % 2):8 * (b % 2) + 8, :] = rbuf[f][k // 32, k % 32]
            if i < 15:
                cp = remote(pbuf.at[f, s], near.at[f, :, t], b_s.at[15 * f + i], b_r.at[16 * f + t], (d, s))
                cp.start()
                waits.append(cp.wait_send)
        cp = pltpu.make_async_copy(pbuf.at[f, t], near.at[f, :, t], b_l.at[f])
        cp.start()
        local.append(cp)

    local = []
    for s in y_peers:
        from_y(s, (0, 1))
    feed(mine, True)
    from_sibling(y, (2, 3))
    feed(2 * y + 1 - c, False)
    second(0)
    from_y(y_peers[0], (2, 3))
    from_y(y_peers[1], (2, 3))
    feed(2 * (y_peers[0] // 4) + c, False)
    feed(2 * (y_peers[1] // 4) + c, False)
    for i in range(2):
        ys = y_peers[i] // 4
        from_sibling(ys, (2, 3))
        feed(2 * ys + 1 - c, False)
    second(1)
    from_y(y_peers[2], (2, 3))
    ys = y_peers[2] // 4
    feed(2 * ys + c, False)
    from_sibling(ys, (2, 3))
    feed(2 * ys + 1 - c, False)
    psend[...] = part[1 - xhi].astype(BF)
    swap = remote(psend, precv, p_s, p_r, (d, flip))
    swap.start()
    second(2)
    for ys in range(4):
        for j, (src, dst) in enumerate(((wqt, wqall), (wo, woall))):
            at = 4 * ys + 2 * (1 - xhi) + c
            remote(src, dst.at[at], h_s.at[0], h_r.at[2 * ys + j], across).wait_recv()
            cp = remote(dst.at[at], dst.at[at], hf_s.at[2 * ys + j], hf_r.at[2 * ys + j], (d, sib))
            cp.start()
            waits.append(cp.wait_send)
    second(3)

    swap.wait()
    enc = (xtok[xhi].astype(F32) + (part[xhi] + precv[...].astype(F32))).astype(BF).astype(F32)
    encoded[...] = enc
    scale = lax.rsqrt(jnp.mean(enc * enc, axis=1, keepdims=True) + 1e-06)
    normed = (enc * scale * gain[...]).astype(BF)
    for ys in range(4):
        from_sibling(ys, (0, 1))
        for j, (src, dst) in enumerate(((wqt, wqall), (wo, woall))):
            at = 4 * ys + 2 * (1 - xhi) + 1 - c
            remote(src, dst.at[at], hf_s.at[0], hf_r.at[2 * ys + j], (d, sib)).wait_recv()
    for e in range(4):
        wpart = wqall[4 * e:4 * e + 4].reshape(256, 1024)
        query[:, 256 * e:256 * e + 256] = (dot(normed, wpart, ((1,), (1,))) * 0.125).astype(BF)

    for f in range(CHUNKS):
        for s in tp_peers:
            remote(pbuf.at[f, s], near.at[f, :, s], b_s.at[0], b_r.at[16 * f + s], (d, s)).wait_recv()
        local[f].wait()
        for n in range(8):
            cols = slice(256 * (n % 4), 256 * (n % 4) + 256)
            full = slice(256 * n, 256 * n + 256)
            wpart = wkvv[n // 4, WIDE * f:WIDE * (f + 1), cols]

            def body(m, carry):
                rows = pl.ds(pl.multiple_of(256 * m, 256), 256)
                term = dot(near[f, m].reshape(256, WIDE), wpart, ((1,), (0,)))
                if f == 0:
                    acc[rows, full] = term
                else:
                    acc[rows, full] += term
                return carry
            lax.fori_loop(0, 4, body, 0)

    lane = lax.broadcasted_iota(jnp.int32, (1, 128), 1)
    low = (lane < 64).astype(F32).astype(BF)
    high = (lane >= 64).astype(F32).astype(BF)
    give = []
    for half in range(2):
        def body(m, carry):
            qrows = pl.ds(pl.multiple_of(64 * m, 64), 64)
            krows = pl.ds(pl.multiple_of(256 * m, 256), 256)
            for pair in range(8):
                cols = slice(128 * pair, 128 * pair + 128)
                vcols = slice(1024 + 128 * pair, 1024 + 128 * pair + 128)
                qp = query[qrows, cols]
                both = jnp.concatenate([qp * low, qp * high], axis=0)
                s = dot(both, acc[krows, cols].astype(BF), ((1,), (1,)))
                e = jnp.exp(s - jnp.max(s, axis=1, keepdims=True))
                total = jnp.sum(e, axis=1, keepdims=True)
                o = dot(e.astype(BF), acc[krows, vcols].astype(BF), ((1,), (0,))) / total
                ctx[qrows, cols] = jnp.where(lane < 64, o[:64], o[64:]).astype(BF)
            return carry
        lax.fori_loop(2 * half, 2 * half + 2, body, 0)
        rows = slice(128 * half, 128 * half + 128)
        for e in range(4):
            cols = slice(256 * e, 256 * e + 256)
            wpart = woall[:, :, cols].reshape(1024, 256)
            m = encoded[rows, cols] + dot(ctx[rows, :], wpart, ((1,), (0,)))
            outt[half, cols, :] = m.T.astype(BF)
        at = pl.ds(pl.multiple_of(256 * t + 128 * half, 128), 128)
        for i, s in enumerate(tp_peers):
            cp = remote(
                outt.at[half, feat(s), :], out.at[:, at],
                g_s.at[15 * half + i], g_r.at[16 * half + t], (d, s))
            cp.start()
            waits.append(cp.wait_send)
        cp = pltpu.make_async_copy(outt.at[half, feat(t), :], out.at[:, at], g_l.at[half])
        cp.start()
        waits.append(cp.wait)
    for half in range(2):
        for s in tp_peers:
            at = pl.ds(pl.multiple_of(256 * s + 128 * half, 128), 128)
            remote(
                outt.at[half, feat(s), :], out.at[:, at],
                g_s.at[0], g_r.at[16 * half + s], (d, s)).wait_recv()
    for w in waits:
        w()


def step(slot, want, gain, qt, up, down, wqt, wo, wkv, base):
    D = pltpu.SemaphoreType.DMA
    V = pltpu.VMEM
    return pl.pallas_call(
        step_kernel,
        name="step",
        out_shape=jax.ShapeDtypeStruct((64, 4096), BF),
        in_specs=[SM, VM, VM, ANY, ANY, ANY, ANY, ANY, ANY, ANY],
        out_specs=ANY,
        scratch_shapes=[
            V((256, 8, 1024), F32),
            V((CHUNKS, 8, 32, 8, WIDE), BF),
            *(V((8, 32, 8, WIDE), BF) for _ in range(CHUNKS)),
            V((CHUNKS, 16, 4, 16, WIDE), BF),
            V((CHUNKS, 4, 16, 16, WIDE), BF),
            V((2, 1024, 256), BF),
            V((2, 256, 1024), BF),
            V((8, 1024, 256), BF),
            V((8, 256, 1024), BF),
            V((16, 64, 1024), BF),
            V((16, 64, 1024), BF),
            V((2, 1024, 1024), BF),
            V((2, 256, 1024), F32),
            V((256, 1024), BF),
            V((256, 1024), BF),
            V((256, 1024), F32),
            V((256, 1024), BF),
            V((1024, 2048), F32),
            V((256, 1024), BF),
            V((2, 1024, 128), BF),
            V((8, 8, 128), jnp.int32),
            pltpu.SMEM((8, 8, 128), jnp.int32),
            D, D((7,)), D((8,)), D((2,)), D((30,)), D((32,)), D((2,)),
            D((12,)), D((16,)), D((5,)), D((16,)), D((16,)),
            D((8,)), D((8,)), D((8,)), D((8,)),
            D((11 * CHUNKS,)), D((16 * CHUNKS,)), D((15 * CHUNKS,)), D((16 * CHUNKS,)), D((CHUNKS,)),
            D, D, D((30,)), D((32,)), D((2,)),
        ],
        compiler_params=pltpu.CompilerParams(
            collective_id=0, has_side_effects=True, vmem_limit_bytes=59 << 20
        ),
    )(slot, want, gain, qt, up, down, wqt, wo, wkv, base)


def per_device(
    queries, enc_up, enc_down, attn_gain, w_query, w_keyval, w_out, database, nb_owner, nb_row
):
    owners = nb_owner.reshape(128)
    rows = nb_row.reshape(128)
    i = jnp.arange(128)
    rank = jnp.sum(
        ((owners[:, None] == owners[None, :]) & (i[None, :] < i[:, None])).astype(jnp.int32), axis=1)
    slot = owners * 32 + rank
    lane = jnp.arange(128)
    key = jnp.where((lane < 32)[None, :], lane[None, :] + 32 * jnp.arange(8)[:, None], -1)
    want = jnp.sum(
        jnp.where(key[:, :, None] == slot[None, None, :], rows[None, None, :], 0), axis=2)
    want = jnp.broadcast_to(want[:, None, :], (8, 8, 128))
    out = step(
        slot, want, attn_gain[None, :], queries.T, enc_up, enc_down, w_query.T, w_out,
        w_keyval, database)
    return out.T


def solution(mesh):
    placed = (
        P("db", "tp"),
        P(None, "tp"),
        P("tp", None),
        P(),
        P(None, "tp"),
        P(),
        P("tp", None),
        P("db", "tp", None),
        P("db", None),
        P("db", None),
    )
    return jax.shard_map(
        per_device, mesh=mesh, in_specs=placed, out_specs=P("db", "tp"), check_vma=False
    )
```

```python
import jax
import jax.numpy as jnp
from jax import lax
from jax.experimental import pallas as pl
from jax.experimental.pallas import tpu as pltpu
from jax.sharding import PartitionSpec as P

MESH = pl.DeviceIdType.MESH
BF = jnp.bfloat16
F32 = jnp.float32
ANY = pl.BlockSpec(memory_space=pl.ANY)
VM = pl.BlockSpec(memory_space=pltpu.VMEM)
SM = pl.BlockSpec(memory_space=pltpu.SMEM)
CHUNKS = 4
WIDE = 1024 // CHUNKS


def remote(src, dst, send, recv, dev):
    return pltpu.make_async_remote_copy(
        src_ref=src, dst_ref=dst, send_sem=send, recv_sem=recv, device_id=dev, device_id_type=MESH
    )


def dot(a, b, dims):
    return lax.dot_general(a, b, (dims, ((), ())), preferred_element_type=F32)


def step_kernel(
    slot, want, gain, qt, up, down, wqt, wo, wkv, base,
    out,
    basev, sbuf, rbuf0, rbuf1, rbuf2, rbuf3, pbuf, near, xbuf, xtok, upall, downall, wqall, woall, wkvv,
    part, psend, precv, encoded, query, acc, ctx, outt, asked, asked_s,
    base_sem, ask_s, ask_r, ask_l, q_s, q_r, q_l, r_s, r_r, w_s, w_r, w_l, f_s, f_r, h_s, h_r, z_s, z_r, hf_s, hf_r,
    a_s, a_r, b_s, b_r, b_l, p_s, p_r, g_s, g_r, g_l,
):
    rbuf = (rbuf0, rbuf1, rbuf2, rbuf3)
    d = lax.axis_index("db")
    t = lax.axis_index("tp")
    xlo, y, xhi, c = d % 2, t // 4, (t // 2) % 2, t % 2
    sib = t + 1 - 2 * c
    flip = t + 2 - 4 * xhi
    load = pltpu.make_async_copy(base, basev, base_sem)
    load.start()
    near_peers = [lax.rem(d + k, 8) for k in (4, 2, 6)]
    lo_peers = [lax.rem(d + k, 8) + 1 - 2 * xlo for k in (4, 2, 6, 0)]
    db_peers = near_peers + lo_peers
    tp_peers = [lax.rem(t + k, 16) for k in range(1, 16)]
    y_peers = [lax.rem(t + 4 * k, 16) for k in (1, 3, 2)]
    across = (d + 1 - 2 * xlo, flip)

    sem = pltpu.get_barrier_semaphore()
    greeted = [(g, t) for g in db_peers] + [(d, s) for s in tp_peers] + [(g, flip) for g in lo_peers]
    for peer in greeted:
        pl.semaphore_signal(sem, inc=1, device_id=peer, device_id_type=MESH)
    pl.semaphore_wait(sem, len(greeted))

    waits = []
    asks = []
    for i, g in enumerate(db_peers):
        cp = remote(want.at[g], asked.at[d], ask_s.at[i], ask_r.at[d], (g, t))
        cp.start()
        asks.append((cp, g))
    own_ask = pltpu.make_async_copy(want.at[d], asked.at[d], ask_l.at[0])
    own_ask.start()

    feat = lambda s: pl.ds(pl.multiple_of(64 * s, 64), 64)
    q_peers = [
        4 * lax.rem(y + k // 2, 4) + 2 * xhi + lax.rem(c + k % 2, 2) for k in range(1, 8)]
    q_at = lambda s: 4 * (s // 4) + 2 * (s % 2)
    for i, s in enumerate(q_peers):
        for p in range(2):
            col = pl.multiple_of(256 * ((s // 4) * 4 + s % 2 + 2 * p), 256)
            cp = remote(
                qt.at[:, pl.ds(col, 256)], xbuf.at[p, feat(t), :],
                q_s.at[2 * i + p], q_r.at[q_at(t) + p], (d, s))
            cp.start()
            waits.append(cp.wait_send)
    own_q = []
    for p in range(2):
        col = pl.multiple_of(256 * (4 * y + c + 2 * p), 256)
        cp = pltpu.make_async_copy(
            qt.at[:, pl.ds(col, 256)], xbuf.at[p, feat(t), :], q_l.at[p])
        cp.start()
        own_q.append(cp)
    mine = 2 * y + c
    weights = lambda ys, core: (
        (wqt, wqall, 4 * ys + 2 * xhi + core), (wo, woall, 4 * ys + 2 * xhi + core),
        (up, upall, 2 * ys + core), (down, downall, 2 * ys + core))
    for j, (src, dst, at) in enumerate(weights(y, c)):
        for i, s in enumerate(y_peers[:2]):
            cp = remote(src, dst.at[at], w_s.at[4 * i + j], w_r.at[4 * y + j], (d, s))
            cp.start()
            waits.append(cp.wait_send)
    own = []
    for j, (src, dst, at) in enumerate(weights(y, c)):
        cp = pltpu.make_async_copy(src, dst.at[at], w_l.at[j])
        cp.start()
        own.append(cp)
        cp = remote(src, dst.at[at], f_s.at[4 * y + j], f_r.at[4 * y + j], (d, sib))
        cp.start()
        waits.append(cp.wait_send)
    cp = pltpu.make_async_copy(wkv, wkvv, w_l.at[4])
    cp.start()
    own.append(cp)

    own_ask.wait()
    for cp, g in asks:
        cp.wait_send()
        remote(want.at[d], asked.at[g], ask_s.at[0], ask_r.at[g], (g, t)).wait_recv()
    to_s = pltpu.make_async_copy(asked, asked_s, ask_l.at[1])
    to_s.start()
    to_s.wait()
    load.wait()

    def pack(f, g, dst):
        def body(r, carry):
            dst[f, g, r] = basev[asked_s[g, 0, r], :, WIDE * f:WIDE * (f + 1)].astype(BF)
            return carry
        lax.fori_loop(0, 32, body, 0, unroll=8)

    def pack_own(f):
        def body(r, carry):
            rbuf[f][d, r] = basev[asked_s[d, 0, r], :, WIDE * f:WIDE * (f + 1)].astype(BF)
            return carry
        lax.fori_loop(0, 32, body, 0, unroll=8)

    def first_pieces(f):
        pieces = [(pl.ds(0, 32), g, t, 0) for g in near_peers]
        for g in lo_peers:
            pieces += [(pl.ds(0, 16), g, t, 0), (pl.ds(16, 16), g, flip, 1)]
        return pieces

    def tokens():
        for k in range(4):
            for p in range(2):
                block = xbuf.at[p, pl.ds(pl.multiple_of(256 * k + 128 * (1 - xhi), 128), 128), :]
                remote(block, block, r_s.at[0], r_r.at[2 * k + p], (d, flip)).wait_recv()
        for p in range(2):
            xtok[p] = xbuf[p].astype(F32).T.astype(BF)

    def feed(at, first):
        def body(p, carry):
            h = dot(xtok[p], upall[at], ((1,), (0,)))
            h = jax.nn.gelu(h, approximate=True).astype(BF)
            term = dot(h, downall[at], ((1,), (0,)))
            if first:
                part[p] = term
            else:
                part[p] += term
            return carry
        lax.fori_loop(0, 2, body, 0)

    def from_sibling(ys, js):
        for j, (src, dst, at) in enumerate(weights(ys, 1 - c)):
            if j in js:
                remote(src, dst.at[at], f_s.at[0], f_r.at[4 * ys + j], (d, sib)).wait_recv()

    def from_y(i, js):
        ys = y_peers[i] // 4
        for j, (src, dst, at) in enumerate(weights(ys, c)):
            if j not in js:
                continue
            remote(src, dst.at[at], w_s.at[0], w_r.at[4 * ys + j], (d, y_peers[i])).wait_recv()
            if i < 2 and j % 2 == i:
                cp = remote(
                    dst.at[at], dst.at[at], w_s.at[8 + j], w_r.at[4 * ys + j], (d, y_peers[1 - i]))
                cp.start()
                waits.append(cp.wait_send)
            cp = remote(dst.at[at], dst.at[at], f_s.at[4 * ys + j], f_r.at[4 * ys + j], (d, sib))
            cp.start()
            waits.append(cp.wait_send)

    def pass_tokens():
        for cp in own_q:
            cp.wait()
        for s in q_peers:
            for p in range(2):
                remote(
                    qt.at[:, pl.ds(0, 256)], xbuf.at[p, feat(s), :],
                    q_s.at[0], q_r.at[q_at(s) + p], (d, s)).wait_recv()
        for k in range(4):
            for p in range(2):
                block = xbuf.at[p, pl.ds(pl.multiple_of(256 * k + 128 * xhi, 128), 128), :]
                cp = remote(block, block, r_s.at[2 * k + p], r_r.at[2 * k + p], (d, flip))
                cp.start()
                waits.append(cp.wait_send)

    z = d // 2
    cross = (wqall, woall)

    def across_send():
        for j, dst in enumerate(cross):
            at = 4 * z + 2 * xhi + c
            cp = remote(dst.at[at], dst.at[at], h_s.at[j], h_r.at[j], across)
            cp.start()
            waits.append(cp.wait_send)

    def to_sibling(zz, j, piece):
        cp = remote(piece, piece, hf_s.at[2 * zz + j], hf_r.at[2 * zz + j], (d, sib))
        cp.start()
        waits.append(cp.wait_send)

    def across_recv():
        for j, dst in enumerate(cross):
            piece = dst.at[4 * z + 2 * (1 - xhi) + c]
            remote(piece, piece, h_s.at[0], h_r.at[j], across).wait_recv()
            for i, g in enumerate(near_peers):
                cp = remote(piece, piece, z_s.at[2 * i + j], z_r.at[2 * z + j], (g, t))
                cp.start()
                waits.append(cp.wait_send)
            to_sibling(z, j, piece)

    def from_z():
        for g in near_peers:
            for j, dst in enumerate(cross):
                piece = dst.at[4 * (g // 2) + 2 * (1 - xhi) + c]
                remote(piece, piece, z_s.at[0], z_r.at[2 * (g // 2) + j], (g, t)).wait_recv()
                to_sibling(g // 2, j, piece)

    def second(f):
        for rows, g, at, half in first_pieces(f):
            remote(
                sbuf.at[f, g, rows], rbuf[f].at[g, rows],
                a_s.at[0], a_r.at[16 * f + 2 * g + half], (g, at)).wait_recv()
        for i, s in enumerate(tp_peers + [t]):
            for b in range(8):
                k = slot[s * 8 + b]
                pbuf[f, s, b // 2, 8 * (b % 2):8 * (b % 2) + 8, :] = rbuf[f][k // 32, k % 32]
            if i < 15:
                cp = remote(pbuf.at[f, s], near.at[f, :, t], b_s.at[15 * f + i], b_r.at[16 * f + t], (d, s))
                cp.start()
                waits.append(cp.wait_send)
        cp = pltpu.make_async_copy(pbuf.at[f, t], near.at[f, :, t], b_l.at[f])
        cp.start()
        local.append(cp)

    def keyval(f):
        for s in tp_peers:
            remote(pbuf.at[f, s], near.at[f, :, s], b_s.at[0], b_r.at[16 * f + s], (d, s)).wait_recv()
        local[f].wait()

        def body(n, carry):
            cols = pl.ds(pl.multiple_of(256 * lax.rem(n, 4), 256), 256)
            full = pl.ds(pl.multiple_of(256 * n, 256), 256)
            wpart = wkvv[n // 4, WIDE * f:WIDE * (f + 1), cols]
            term = dot(near[f].reshape(1024, WIDE), wpart, ((1,), (0,)))
            if f == 0:
                acc[:, full] = term
            else:
                acc[:, full] += term
            return carry
        lax.fori_loop(0, 8, body, 0)

    for f in range(CHUNKS):
        n = 0
        for k, g in enumerate(db_peers):
            pack(f, g, sbuf)
            for rows, to, at, half in first_pieces(f):
                if to is g:
                    cp = remote(
                        sbuf.at[f, g, rows], rbuf[f].at[d, rows],
                        a_s.at[11 * f + n], a_r.at[16 * f + 2 * d + half], (g, at))
                    cp.start()
                    waits.append(cp.wait_send)
                    n += 1
        pack_own(f)
        if f == 0:
            pass_tokens()

    local = []
    ys = [s // 4 for s in y_peers]
    for cp in own:
        cp.wait()
    from_y(0, (0, 1))
    from_y(1, (0, 1))
    second(0)
    from_y(2, (0, 1))
    across_send()
    tokens()
    feed(mine, True)
    from_sibling(y, (2, 3))
    feed(2 * y + 1 - c, False)
    second(1)
    from_y(0, (2, 3))
    from_y(1, (2, 3))
    across_recv()
    feed(2 * ys[0] + c, False)
    feed(2 * ys[1] + c, False)
    second(2)
    keyval(0)
    for i in range(2):
        from_sibling(ys[i], (2, 3))
        feed(2 * ys[i] + 1 - c, False)
    from_z()
    from_y(2, (2, 3))
    second(3)
    feed(2 * ys[2] + c, False)
    from_sibling(ys[2], (2, 3))
    feed(2 * ys[2] + 1 - c, False)
    psend[...] = part[1 - xhi].astype(BF)
    swap = remote(psend, precv, p_s, p_r, (d, flip))
    swap.start()
    keyval(1)
    keyval(2)

    swap.wait()
    enc = (xtok[xhi].astype(F32) + (part[xhi] + precv[...].astype(F32))).astype(BF).astype(F32)
    encoded[...] = enc
    scale = lax.rsqrt(jnp.mean(enc * enc, axis=1, keepdims=True) + 1e-06)
    normed = (enc * scale * gain[...]).astype(BF)
    for k in range(4):
        from_sibling(k, (0, 1))
        for j, (src, dst) in enumerate(((wqt, wqall), (wo, woall))):
            at = 4 * k + 2 * (1 - xhi) + 1 - c
            remote(src, dst.at[at], hf_s.at[0], hf_r.at[2 * k + j], (d, sib)).wait_recv()
    for e in range(4):
        wpart = wqall[4 * e:4 * e + 4].reshape(256, 1024)
        query[:, 256 * e:256 * e + 256] = (dot(normed, wpart, ((1,), (1,))) * 0.125).astype(BF)

    keyval(3)
    lane = lax.broadcasted_iota(jnp.int32, (1, 128), 1)
    low = (lane < 64).astype(F32).astype(BF)
    high = (lane >= 64).astype(F32).astype(BF)
    give = []
    for half in range(2):
        def body(m, carry):
            qrows = pl.ds(pl.multiple_of(64 * m, 64), 64)
            krows = pl.ds(pl.multiple_of(256 * m, 256), 256)
            for pair in range(8):
                cols = slice(128 * pair, 128 * pair + 128)
                vcols = slice(1024 + 128 * pair, 1024 + 128 * pair + 128)
                qp = query[qrows, cols]
                both = jnp.concatenate([qp * low, qp * high], axis=0)
                s = dot(both, acc[krows, cols].astype(BF), ((1,), (1,)))
                e = jnp.exp(s - jnp.max(s, axis=1, keepdims=True))
                total = jnp.sum(e, axis=1, keepdims=True)
                o = dot(e.astype(BF), acc[krows, vcols].astype(BF), ((1,), (0,))) / total
                ctx[qrows, cols] = jnp.where(lane < 64, o[:64], o[64:]).astype(BF)
            return carry
        lax.fori_loop(2 * half, 2 * half + 2, body, 0)
        rows = slice(128 * half, 128 * half + 128)
        for e in range(4):
            cols = slice(256 * e, 256 * e + 256)
            wpart = woall[:, :, cols].reshape(1024, 256)
            m = encoded[rows, cols] + dot(ctx[rows, :], wpart, ((1,), (0,)))
            outt[half, cols, :] = m.T.astype(BF)
        at = pl.ds(pl.multiple_of(256 * t + 128 * half, 128), 128)
        for i, s in enumerate(tp_peers):
            cp = remote(
                outt.at[half, feat(s), :], out.at[:, at],
                g_s.at[15 * half + i], g_r.at[16 * half + t], (d, s))
            cp.start()
            waits.append(cp.wait_send)
        cp = pltpu.make_async_copy(outt.at[half, feat(t), :], out.at[:, at], g_l.at[half])
        cp.start()
        waits.append(cp.wait)
    for half in range(2):
        for s in tp_peers:
            at = pl.ds(pl.multiple_of(256 * s + 128 * half, 128), 128)
            remote(
                outt.at[half, feat(s), :], out.at[:, at],
                g_s.at[0], g_r.at[16 * half + s], (d, s)).wait_recv()
    for w in waits:
        w()


def step(slot, want, gain, qt, up, down, wqt, wo, wkv, base):
    D = pltpu.SemaphoreType.DMA
    V = pltpu.VMEM
    return pl.pallas_call(
        step_kernel,
        name="step",
        out_shape=jax.ShapeDtypeStruct((64, 4096), BF),
        in_specs=[SM, VM, VM, ANY, ANY, ANY, ANY, ANY, ANY, ANY],
        out_specs=ANY,
        scratch_shapes=[
            V((256, 8, 1024), F32),
            V((CHUNKS, 8, 32, 8, WIDE), BF),
            *(V((8, 32, 8, WIDE), BF) for _ in range(CHUNKS)),
            V((CHUNKS, 16, 4, 16, WIDE), BF),
            V((CHUNKS, 4, 16, 16, WIDE), BF),
            V((2, 1024, 256), BF),
            V((2, 256, 1024), BF),
            V((8, 1024, 256), BF),
            V((8, 256, 1024), BF),
            V((16, 64, 1024), BF),
            V((16, 64, 1024), BF),
            V((2, 1024, 1024), BF),
            V((2, 256, 1024), F32),
            V((256, 1024), BF),
            V((256, 1024), BF),
            V((256, 1024), F32),
            V((256, 1024), BF),
            V((1024, 2048), F32),
            V((256, 1024), BF),
            V((2, 1024, 128), BF),
            V((8, 8, 128), jnp.int32),
            pltpu.SMEM((8, 8, 128), jnp.int32),
            D, D((7,)), D((8,)), D((2,)), D((14,)), D((16,)), D((2,)), D((8,)), D((8,)),
            D((12,)), D((16,)), D((5,)), D((16,)), D((16,)),
            D((2,)), D((2,)), D((6,)), D((8,)), D((8,)), D((8,)),
            D((11 * CHUNKS,)), D((16 * CHUNKS,)), D((15 * CHUNKS,)), D((16 * CHUNKS,)), D((CHUNKS,)),
            D, D, D((30,)), D((32,)), D((2,)),
        ],
        compiler_params=pltpu.CompilerParams(
            collective_id=0, has_side_effects=True, vmem_limit_bytes=59 << 20
        ),
    )(slot, want, gain, qt, up, down, wqt, wo, wkv, base)


def per_device(
    queries, enc_up, enc_down, attn_gain, w_query, w_keyval, w_out, database, nb_owner, nb_row
):
    owners = nb_owner.reshape(128)
    rows = nb_row.reshape(128)
    i = jnp.arange(128)
    rank = jnp.sum(
        ((owners[:, None] == owners[None, :]) & (i[None, :] < i[:, None])).astype(jnp.int32), axis=1)
    slot = owners * 32 + rank
    lane = jnp.arange(128)
    key = jnp.where((lane < 32)[None, :], lane[None, :] + 32 * jnp.arange(8)[:, None], -1)
    want = jnp.sum(
        jnp.where(key[:, :, None] == slot[None, None, :], rows[None, None, :], 0), axis=2)
    want = jnp.broadcast_to(want[:, None, :], (8, 8, 128))
    out = step(
        slot, want, attn_gain[None, :], queries.T, enc_up, enc_down, w_query.T, w_out,
        w_keyval, database)
    return out.T


def solution(mesh):
    placed = (
        P("db", "tp"),
        P(None, "tp"),
        P("tp", None),
        P(),
        P(None, "tp"),
        P(),
        P("tp", None),
        P("db", "tp", None),
        P("db", None),
        P("db", None),
    )
    return jax.shard_map(
        per_device, mesh=mesh, in_specs=placed, out_specs=P("db", "tp"), check_vma=False
    )
```

```python
import jax
import jax.numpy as jnp
from jax import lax
from jax.experimental import pallas as pl
from jax.experimental.pallas import tpu as pltpu
from jax.sharding import PartitionSpec as P

MESH = pl.DeviceIdType.MESH
BF = jnp.bfloat16
F32 = jnp.float32
ANY = pl.BlockSpec(memory_space=pl.ANY)
VM = pl.BlockSpec(memory_space=pltpu.VMEM)
SM = pl.BlockSpec(memory_space=pltpu.SMEM)
CHUNKS = 4
WIDE = 1024 // CHUNKS


def remote(src, dst, send, recv, dev):
    return pltpu.make_async_remote_copy(
        src_ref=src, dst_ref=dst, send_sem=send, recv_sem=recv, device_id=dev, device_id_type=MESH
    )


def dot(a, b, dims):
    return lax.dot_general(a, b, (dims, ((), ())), preferred_element_type=F32)


def step_kernel(
    slot, want, gain, qt, up, down, wqt, wo, wkv, base,
    out,
    basev, sbuf, rbuf0, rbuf1, rbuf2, rbuf3, pbuf, near, xbuf, xtok, upall, downall, wqall, woall, wkvv,
    part, psend, precv, encoded, query, acc, ctx, outt, asked, asked_s,
    base_sem, ask_s, ask_r, ask_l, q_s, q_r, q_l, r_s, r_r, w_s, w_r, w_l, f_s, f_r, h_s, h_r, z_s, z_r, hf_s, hf_r,
    a_s, a_r, b_s, b_r, b_l, p_s, p_r, g_s, g_r, g_l,
):
    rbuf = (rbuf0, rbuf1, rbuf2, rbuf3)
    d = lax.axis_index("db")
    t = lax.axis_index("tp")
    xlo, y, xhi, c = d % 2, t // 4, (t // 2) % 2, t % 2
    sib = t + 1 - 2 * c
    flip = t + 2 - 4 * xhi
    load = pltpu.make_async_copy(base, basev, base_sem)
    load.start()
    near_peers = [lax.rem(d + k, 8) for k in (4, 2, 6)]
    lo_peers = [lax.rem(d + k, 8) + 1 - 2 * xlo for k in (4, 2, 6, 0)]
    db_peers = near_peers + lo_peers
    tp_peers = [lax.rem(t + k, 16) for k in range(1, 16)]
    y_peers = [lax.rem(t + 4 * k, 16) for k in (1, 3, 2)]
    across = (d + 1 - 2 * xlo, flip)

    sem = pltpu.get_barrier_semaphore()
    greeted = [(g, t) for g in db_peers] + [(d, s) for s in tp_peers] + [(g, flip) for g in lo_peers]
    for peer in greeted:
        pl.semaphore_signal(sem, inc=1, device_id=peer, device_id_type=MESH)
    pl.semaphore_wait(sem, len(greeted))

    waits = []
    asks = []
    for i, g in enumerate(db_peers):
        cp = remote(want.at[g], asked.at[d], ask_s.at[i], ask_r.at[d], (g, t))
        cp.start()
        asks.append((cp, g))
    own_ask = pltpu.make_async_copy(want.at[d], asked.at[d], ask_l.at[0])
    own_ask.start()

    feat = lambda s: pl.ds(pl.multiple_of(64 * s, 64), 64)
    q_peers = [
        4 * lax.rem(y + k // 2, 4) + 2 * xhi + lax.rem(c + k % 2, 2) for k in range(1, 8)]
    q_at = lambda s: 4 * (s // 4) + 2 * (s % 2)
    for i, s in enumerate(q_peers):
        for p in range(2):
            col = pl.multiple_of(256 * ((s // 4) * 4 + s % 2 + 2 * p), 256)
            cp = remote(
                qt.at[:, pl.ds(col, 256)], xbuf.at[p, feat(t), :],
                q_s.at[2 * i + p], q_r.at[q_at(t) + p], (d, s))
            cp.start()
            waits.append(cp.wait_send)
    own_q = []
    for p in range(2):
        col = pl.multiple_of(256 * (4 * y + c + 2 * p), 256)
        cp = pltpu.make_async_copy(
            qt.at[:, pl.ds(col, 256)], xbuf.at[p, feat(t), :], q_l.at[p])
        cp.start()
        own_q.append(cp)
    mine = 2 * y + c
    weights = lambda ys, core: (
        (wqt, wqall, 4 * ys + 2 * xhi + core), (wo, woall, 4 * ys + 2 * xhi + core),
        (up, upall, 2 * ys + core), (down, downall, 2 * ys + core))
    for i, j in ((0, 1), (1, 0), (0, 0), (1, 1), (0, 3), (1, 2), (0, 2), (1, 3)):
        src, dst, at = weights(y, c)[j]
        cp = remote(src, dst.at[at], w_s.at[4 * i + j], w_r.at[4 * y + j], (d, y_peers[i]))
        cp.start()
        waits.append(cp.wait_send)
    own = []
    for j, (src, dst, at) in enumerate(weights(y, c)):
        cp = pltpu.make_async_copy(src, dst.at[at], w_l.at[j])
        cp.start()
        own.append(cp)
        cp = remote(src, dst.at[at], f_s.at[4 * y + j], f_r.at[4 * y + j], (d, sib))
        cp.start()
        waits.append(cp.wait_send)
    cp = pltpu.make_async_copy(wkv, wkvv, w_l.at[4])
    cp.start()
    own.append(cp)

    own_ask.wait()
    for cp, g in asks:
        cp.wait_send()
        remote(want.at[d], asked.at[g], ask_s.at[0], ask_r.at[g], (g, t)).wait_recv()
    to_s = pltpu.make_async_copy(asked, asked_s, ask_l.at[1])
    to_s.start()
    to_s.wait()
    load.wait()

    def pack(f, g, dst):
        def body(r, carry):
            dst[f, g, r] = basev[asked_s[g, 0, r], :, WIDE * f:WIDE * (f + 1)].astype(BF)
            return carry
        lax.fori_loop(0, 32, body, 0, unroll=8)

    def pack_own(f):
        def body(r, carry):
            rbuf[f][d, r] = basev[asked_s[d, 0, r], :, WIDE * f:WIDE * (f + 1)].astype(BF)
            return carry
        lax.fori_loop(0, 32, body, 0, unroll=8)

    def first_pieces(f):
        pieces = [(pl.ds(0, 32), g, t, 0) for g in near_peers]
        for g in lo_peers:
            pieces += [(pl.ds(0, 16), g, t, 0), (pl.ds(16, 16), g, flip, 1)]
        return pieces

    def tokens():
        for k in range(4):
            for p in range(2):
                block = xbuf.at[p, pl.ds(pl.multiple_of(256 * k + 128 * (1 - xhi), 128), 128), :]
                remote(block, block, r_s.at[0], r_r.at[2 * k + p], (d, flip)).wait_recv()
        for p in range(2):
            xtok[p] = xbuf[p].astype(F32).T.astype(BF)

    def feed(at, first):
        def body(p, carry):
            h = dot(xtok[p], upall[at], ((1,), (0,)))
            h = jax.nn.gelu(h, approximate=True).astype(BF)
            term = dot(h, downall[at], ((1,), (0,)))
            if first:
                part[p] = term
            else:
                part[p] += term
            return carry
        lax.fori_loop(0, 2, body, 0)

    def from_sibling(ys, js):
        for j, (src, dst, at) in enumerate(weights(ys, 1 - c)):
            if j in js:
                remote(src, dst.at[at], f_s.at[0], f_r.at[4 * ys + j], (d, sib)).wait_recv()

    def from_y(i, js):
        ys = y_peers[i] // 4
        for j, (src, dst, at) in enumerate(weights(ys, c)):
            if j not in js:
                continue
            remote(src, dst.at[at], w_s.at[0], w_r.at[4 * ys + j], (d, y_peers[i])).wait_recv()
            if i < 2 and j % 2 == i:
                cp = remote(
                    dst.at[at], dst.at[at], w_s.at[8 + j], w_r.at[4 * ys + j], (d, y_peers[1 - i]))
                cp.start()
                waits.append(cp.wait_send)
            cp = remote(dst.at[at], dst.at[at], f_s.at[4 * ys + j], f_r.at[4 * ys + j], (d, sib))
            cp.start()
            waits.append(cp.wait_send)

    def pass_tokens():
        for cp in own_q:
            cp.wait()
        for s in q_peers:
            for p in range(2):
                remote(
                    qt.at[:, pl.ds(0, 256)], xbuf.at[p, feat(s), :],
                    q_s.at[0], q_r.at[q_at(s) + p], (d, s)).wait_recv()
        for k in range(4):
            for p in range(2):
                block = xbuf.at[p, pl.ds(pl.multiple_of(256 * k + 128 * xhi, 128), 128), :]
                cp = remote(block, block, r_s.at[2 * k + p], r_r.at[2 * k + p], (d, flip))
                cp.start()
                waits.append(cp.wait_send)

    z = d // 2
    cross = (wqall, woall)

    def across_send():
        for j, dst in enumerate(cross):
            at = 4 * z + 2 * xhi + c
            cp = remote(dst.at[at], dst.at[at], h_s.at[j], h_r.at[j], across)
            cp.start()
            waits.append(cp.wait_send)

    def to_sibling(zz, j, piece):
        cp = remote(piece, piece, hf_s.at[2 * zz + j], hf_r.at[2 * zz + j], (d, sib))
        cp.start()
        waits.append(cp.wait_send)

    def across_recv():
        for j, dst in enumerate(cross):
            piece = dst.at[4 * z + 2 * (1 - xhi) + c]
            remote(piece, piece, h_s.at[0], h_r.at[j], across).wait_recv()
            for i, g in enumerate(near_peers):
                cp = remote(piece, piece, z_s.at[2 * i + j], z_r.at[2 * z + j], (g, t))
                cp.start()
                waits.append(cp.wait_send)
            to_sibling(z, j, piece)

    def from_z():
        for g in near_peers:
            for j, dst in enumerate(cross):
                piece = dst.at[4 * (g // 2) + 2 * (1 - xhi) + c]
                remote(piece, piece, z_s.at[0], z_r.at[2 * (g // 2) + j], (g, t)).wait_recv()
                to_sibling(g // 2, j, piece)

    def second(f):
        for rows, g, at, half in first_pieces(f):
            remote(
                sbuf.at[f, g, rows], rbuf[f].at[g, rows],
                a_s.at[0], a_r.at[16 * f + 2 * g + half], (g, at)).wait_recv()
        for i, s in enumerate(tp_peers + [t]):
            for b in range(8):
                k = slot[s * 8 + b]
                pbuf[f, s, b // 2, 8 * (b % 2):8 * (b % 2) + 8, :] = rbuf[f][k // 32, k % 32]
            if i < 15:
                cp = remote(pbuf.at[f, s], near.at[f, :, t], b_s.at[15 * f + i], b_r.at[16 * f + t], (d, s))
                cp.start()
                waits.append(cp.wait_send)
        cp = pltpu.make_async_copy(pbuf.at[f, t], near.at[f, :, t], b_l.at[f])
        cp.start()
        local.append(cp)

    def keyval(f):
        for s in tp_peers:
            remote(pbuf.at[f, s], near.at[f, :, s], b_s.at[0], b_r.at[16 * f + s], (d, s)).wait_recv()
        local[f].wait()

        def body(n, carry):
            cols = pl.ds(pl.multiple_of(512 * lax.rem(n, 2), 512), 512)
            full = pl.ds(pl.multiple_of(512 * n, 512), 512)
            wpart = wkvv[n // 2, WIDE * f:WIDE * (f + 1), cols]
            term = dot(near[f].reshape(1024, WIDE), wpart, ((1,), (0,)))
            if f == 0:
                acc[:, full] = term
            else:
                acc[:, full] += term
            return carry
        lax.fori_loop(0, 4, body, 0)

    for f in range(CHUNKS):
        n = 0
        for k, g in enumerate(db_peers):
            pack(f, g, sbuf)
            for rows, to, at, half in first_pieces(f):
                if to is g:
                    cp = remote(
                        sbuf.at[f, g, rows], rbuf[f].at[d, rows],
                        a_s.at[11 * f + n], a_r.at[16 * f + 2 * d + half], (g, at))
                    cp.start()
                    waits.append(cp.wait_send)
                    n += 1
        pack_own(f)
        if f == 0:
            pass_tokens()

    local = []
    ys = [s // 4 for s in y_peers]
    for cp in own:
        cp.wait()
    from_y(0, (0, 1))
    from_y(1, (0, 1))
    second(0)
    from_y(2, (0, 1))
    across_send()
    from_y(0, (2,))
    from_y(1, (3,))
    tokens()
    feed(mine, True)
    from_sibling(y, (2, 3))
    feed(2 * y + 1 - c, False)
    second(1)
    from_y(0, (3,))
    from_y(1, (2,))
    across_recv()
    feed(2 * ys[0] + c, False)
    feed(2 * ys[1] + c, False)
    second(2)
    for i in range(2):
        from_sibling(ys[i], (2, 3))
        feed(2 * ys[i] + 1 - c, False)
    from_z()
    from_y(2, (2, 3))
    second(3)
    feed(2 * ys[2] + c, False)
    from_sibling(ys[2], (2, 3))
    feed(2 * ys[2] + 1 - c, False)
    psend[...] = part[1 - xhi].astype(BF)
    swap = remote(psend, precv, p_s, p_r, (d, flip))
    swap.start()
    keyval(0)
    keyval(1)
    keyval(2)

    swap.wait()
    enc = (xtok[xhi].astype(F32) + (part[xhi] + precv[...].astype(F32))).astype(BF).astype(F32)
    encoded[...] = enc
    scale = lax.rsqrt(jnp.mean(enc * enc, axis=1, keepdims=True) + 1e-06)
    normed = (enc * scale * gain[...]).astype(BF)
    for k in range(4):
        from_sibling(k, (0, 1))
        for j, (src, dst) in enumerate(((wqt, wqall), (wo, woall))):
            at = 4 * k + 2 * (1 - xhi) + 1 - c
            remote(src, dst.at[at], hf_s.at[0], hf_r.at[2 * k + j], (d, sib)).wait_recv()
    for e in range(4):
        wpart = wqall[4 * e:4 * e + 4].reshape(256, 1024)
        query[:, 256 * e:256 * e + 256] = (dot(normed, wpart, ((1,), (1,))) * 0.125).astype(BF)

    keyval(3)
    lane = lax.broadcasted_iota(jnp.int32, (1, 128), 1)
    low = (lane < 64).astype(F32).astype(BF)
    high = (lane >= 64).astype(F32).astype(BF)
    give = []
    for half in range(2):
        def body(m, carry):
            qrows = pl.ds(pl.multiple_of(64 * m, 64), 64)
            krows = pl.ds(pl.multiple_of(256 * m, 256), 256)
            for pair in range(8):
                cols = slice(128 * pair, 128 * pair + 128)
                vcols = slice(1024 + 128 * pair, 1024 + 128 * pair + 128)
                qp = query[qrows, cols]
                both = jnp.concatenate([qp * low, qp * high], axis=0)
                s = dot(both, acc[krows, cols].astype(BF), ((1,), (1,)))
                e = jnp.exp(s - jnp.max(s, axis=1, keepdims=True))
                total = jnp.sum(e, axis=1, keepdims=True)
                o = dot(e.astype(BF), acc[krows, vcols].astype(BF), ((1,), (0,))) / total
                ctx[qrows, cols] = jnp.where(lane < 64, o[:64], o[64:]).astype(BF)
            return carry
        lax.fori_loop(2 * half, 2 * half + 2, body, 0)
        rows = slice(128 * half, 128 * half + 128)
        for e in range(4):
            cols = slice(256 * e, 256 * e + 256)
            wpart = woall[:, :, cols].reshape(1024, 256)
            m = encoded[rows, cols] + dot(ctx[rows, :], wpart, ((1,), (0,)))
            outt[half, cols, :] = m.T.astype(BF)
        at = pl.ds(pl.multiple_of(256 * t + 128 * half, 128), 128)
        for i, s in enumerate(tp_peers):
            cp = remote(
                outt.at[half, feat(s), :], out.at[:, at],
                g_s.at[15 * half + i], g_r.at[16 * half + t], (d, s))
            cp.start()
            waits.append(cp.wait_send)
        cp = pltpu.make_async_copy(outt.at[half, feat(t), :], out.at[:, at], g_l.at[half])
        cp.start()
        waits.append(cp.wait)
    for half in range(2):
        for s in tp_peers:
            at = pl.ds(pl.multiple_of(256 * s + 128 * half, 128), 128)
            remote(
                outt.at[half, feat(s), :], out.at[:, at],
                g_s.at[0], g_r.at[16 * half + s], (d, s)).wait_recv()
    for w in waits:
        w()


def step(slot, want, gain, qt, up, down, wqt, wo, wkv, base):
    D = pltpu.SemaphoreType.DMA
    V = pltpu.VMEM
    return pl.pallas_call(
        step_kernel,
        name="step",
        out_shape=jax.ShapeDtypeStruct((64, 4096), BF),
        in_specs=[SM, VM, VM, ANY, ANY, ANY, ANY, ANY, ANY, ANY],
        out_specs=ANY,
        scratch_shapes=[
            V((256, 8, 1024), F32),
            V((CHUNKS, 8, 32, 8, WIDE), BF),
            *(V((8, 32, 8, WIDE), BF) for _ in range(CHUNKS)),
            V((CHUNKS, 16, 4, 16, WIDE), BF),
            V((CHUNKS, 4, 16, 16, WIDE), BF),
            V((2, 1024, 256), BF),
            V((2, 256, 1024), BF),
            V((8, 1024, 256), BF),
            V((8, 256, 1024), BF),
            V((16, 64, 1024), BF),
            V((16, 64, 1024), BF),
            V((2, 1024, 1024), BF),
            V((2, 256, 1024), F32),
            V((256, 1024), BF),
            V((256, 1024), BF),
            V((256, 1024), F32),
            V((256, 1024), BF),
            V((1024, 2048), F32),
            V((256, 1024), BF),
            V((2, 1024, 128), BF),
            V((8, 8, 128), jnp.int32),
            pltpu.SMEM((8, 8, 128), jnp.int32),
            D, D((7,)), D((8,)), D((2,)), D((14,)), D((16,)), D((2,)), D((8,)), D((8,)),
            D((12,)), D((16,)), D((5,)), D((16,)), D((16,)),
            D((2,)), D((2,)), D((6,)), D((8,)), D((8,)), D((8,)),
            D((11 * CHUNKS,)), D((16 * CHUNKS,)), D((15 * CHUNKS,)), D((16 * CHUNKS,)), D((CHUNKS,)),
            D, D, D((30,)), D((32,)), D((2,)),
        ],
        compiler_params=pltpu.CompilerParams(
            collective_id=0, has_side_effects=True, vmem_limit_bytes=59 << 20
        ),
    )(slot, want, gain, qt, up, down, wqt, wo, wkv, base)


def per_device(
    queries, enc_up, enc_down, attn_gain, w_query, w_keyval, w_out, database, nb_owner, nb_row
):
    owners = nb_owner.reshape(128)
    rows = nb_row.reshape(128)
    i = jnp.arange(128)
    rank = jnp.sum(
        ((owners[:, None] == owners[None, :]) & (i[None, :] < i[:, None])).astype(jnp.int32), axis=1)
    slot = owners * 32 + rank
    lane = jnp.arange(128)
    key = jnp.where((lane < 32)[None, :], lane[None, :] + 32 * jnp.arange(8)[:, None], -1)
    want = jnp.sum(
        jnp.where(key[:, :, None] == slot[None, None, :], rows[None, None, :], 0), axis=2)
    want = jnp.broadcast_to(want[:, None, :], (8, 8, 128))
    out = step(
        slot, want, attn_gain[None, :], queries.T, enc_up, enc_down, w_query.T, w_out,
        w_keyval, database)
    return out.T


def solution(mesh):
    placed = (
        P("db", "tp"),
        P(None, "tp"),
        P("tp", None),
        P(),
        P(None, "tp"),
        P(),
        P("tp", None),
        P("db", "tp", None),
        P("db", None),
        P("db", None),
    )
    return jax.shard_map(
        per_device, mesh=mesh, in_specs=placed, out_specs=P("db", "tp"), check_vma=False
    )
```

```python
import jax
import jax.numpy as jnp
from jax import lax
from jax.experimental import pallas as pl
from jax.experimental.pallas import tpu as pltpu
from jax.sharding import PartitionSpec as P

MESH = pl.DeviceIdType.MESH
BF = jnp.bfloat16
F32 = jnp.float32
ANY = pl.BlockSpec(memory_space=pl.ANY)
VM = pl.BlockSpec(memory_space=pltpu.VMEM)
SM = pl.BlockSpec(memory_space=pltpu.SMEM)
CHUNKS = 4
WIDE = 1024 // CHUNKS


def remote(src, dst, send, recv, dev):
    return pltpu.make_async_remote_copy(
        src_ref=src, dst_ref=dst, send_sem=send, recv_sem=recv, device_id=dev, device_id_type=MESH
    )


def dot(a, b, dims):
    return lax.dot_general(a, b, (dims, ((), ())), preferred_element_type=F32)


def step_kernel(
    slot, want, gain, qt, up, down, wqt, wo, wkv, base,
    out,
    basev, sbuf, rbuf0, rbuf1, rbuf2, rbuf3, pbuf, near, xbuf, xtok, upall, downall, wqall, woall, wkvv,
    part, psend, precv, encoded, query, acc, ctx, outt, asked, asked_s,
    base_sem, ask_s, ask_r, ask_l, q_s, q_r, q_l, r_s, r_r, w_s, w_r, w_l, f_s, f_r, h_s, h_r, z_s, z_r, hf_s, hf_r,
    a_s, a_r, b_s, b_r, b_l, p_s, p_r, g_s, g_r, g_l,
):
    rbuf = (rbuf0, rbuf1, rbuf2, rbuf3)
    d = lax.axis_index("db")
    t = lax.axis_index("tp")
    xlo, y, xhi, c = d % 2, t // 4, (t // 2) % 2, t % 2
    sib = t + 1 - 2 * c
    flip = t + 2 - 4 * xhi
    load = pltpu.make_async_copy(base, basev, base_sem)
    load.start()
    near_peers = [lax.rem(d + k, 8) for k in (4, 2, 6)]
    lo_peers = [lax.rem(d + k, 8) + 1 - 2 * xlo for k in (4, 2, 6, 0)]
    db_peers = near_peers + lo_peers
    tp_peers = [lax.rem(t + k, 16) for k in range(1, 16)]
    y_peers = [lax.rem(t + 4 * k, 16) for k in (1, 3, 2)]
    across = (d + 1 - 2 * xlo, flip)

    sem = pltpu.get_barrier_semaphore()
    greeted = [(g, t) for g in db_peers] + [(d, s) for s in tp_peers] + [(g, flip) for g in lo_peers]
    for peer in greeted:
        pl.semaphore_signal(sem, inc=1, device_id=peer, device_id_type=MESH)
    pl.semaphore_wait(sem, len(greeted))

    waits = []
    asks = []
    for i, g in enumerate(db_peers):
        cp = remote(want.at[g], asked.at[d], ask_s.at[i], ask_r.at[d], (g, t))
        cp.start()
        asks.append((cp, g))
    own_ask = pltpu.make_async_copy(want.at[d], asked.at[d], ask_l.at[0])
    own_ask.start()

    feat = lambda s: pl.ds(pl.multiple_of(64 * s, 64), 64)
    q_peers = [
        4 * lax.rem(y + k // 2, 4) + 2 * xhi + lax.rem(c + k % 2, 2) for k in range(1, 8)]
    q_at = lambda s: 4 * (s // 4) + 2 * (s % 2)
    for i, s in enumerate(q_peers):
        for p in range(2):
            col = pl.multiple_of(256 * ((s // 4) * 4 + s % 2 + 2 * p), 256)
            cp = remote(
                qt.at[:, pl.ds(col, 256)], xbuf.at[p, feat(t), :],
                q_s.at[2 * i + p], q_r.at[q_at(t) + p], (d, s))
            cp.start()
            waits.append(cp.wait_send)
    own_q = []
    for p in range(2):
        col = pl.multiple_of(256 * (4 * y + c + 2 * p), 256)
        cp = pltpu.make_async_copy(
            qt.at[:, pl.ds(col, 256)], xbuf.at[p, feat(t), :], q_l.at[p])
        cp.start()
        own_q.append(cp)
    mine = 2 * y + c
    weights = lambda ys, core: (
        (wqt, wqall, 4 * ys + 2 * xhi + core), (wo, woall, 4 * ys + 2 * xhi + core),
        (up, upall, 2 * ys + core), (down, downall, 2 * ys + core))
    for i, j in ((0, 1), (1, 0), (0, 0), (1, 1), (0, 3), (1, 2), (0, 2), (1, 3)):
        src, dst, at = weights(y, c)[j]
        cp = remote(src, dst.at[at], w_s.at[4 * i + j], w_r.at[4 * y + j], (d, y_peers[i]))
        cp.start()
        waits.append(cp.wait_send)
    own = []
    for j, (src, dst, at) in enumerate(weights(y, c)):
        cp = pltpu.make_async_copy(src, dst.at[at], w_l.at[j])
        cp.start()
        own.append(cp)
        cp = remote(src, dst.at[at], f_s.at[4 * y + j], f_r.at[4 * y + j], (d, sib))
        cp.start()
        waits.append(cp.wait_send)
    cp = pltpu.make_async_copy(wkv, wkvv, w_l.at[4])
    cp.start()
    own.append(cp)

    own_ask.wait()
    for cp, g in asks:
        cp.wait_send()
        remote(want.at[d], asked.at[g], ask_s.at[0], ask_r.at[g], (g, t)).wait_recv()
    to_s = pltpu.make_async_copy(asked, asked_s, ask_l.at[1])
    to_s.start()
    to_s.wait()
    load.wait()

    def pack(f, g, dst):
        def body(r, carry):
            dst[f, g, r] = basev[asked_s[g, 0, r], :, WIDE * f:WIDE * (f + 1)].astype(BF)
            return carry
        lax.fori_loop(0, 32, body, 0, unroll=8)

    def pack_own(f):
        def body(r, carry):
            rbuf[f][d, r] = basev[asked_s[d, 0, r], :, WIDE * f:WIDE * (f + 1)].astype(BF)
            return carry
        lax.fori_loop(0, 32, body, 0, unroll=8)

    def first_pieces(f):
        pieces = [(pl.ds(0, 32), g, t, 0) for g in near_peers]
        for g in lo_peers:
            pieces += [(pl.ds(0, 16), g, t, 0), (pl.ds(16, 16), g, flip, 1)]
        return pieces

    def tokens():
        for k in range(4):
            for p in range(2):
                block = xbuf.at[p, pl.ds(pl.multiple_of(256 * k + 128 * (1 - xhi), 128), 128), :]
                remote(block, block, r_s.at[0], r_r.at[2 * k + p], (d, flip)).wait_recv()
        for p in range(2):
            xtok[p] = xbuf[p].astype(F32).T.astype(BF)

    def feed(at, first):
        def body(p, carry):
            h = dot(xtok[p], upall[at], ((1,), (0,)))
            h = jax.nn.gelu(h, approximate=True).astype(BF)
            term = dot(h, downall[at], ((1,), (0,)))
            if first:
                part[p] = term
            else:
                part[p] += term
            return carry
        lax.fori_loop(0, 2, body, 0)

    def from_sibling(ys, js):
        for j, (src, dst, at) in enumerate(weights(ys, 1 - c)):
            if j in js:
                remote(src, dst.at[at], f_s.at[0], f_r.at[4 * ys + j], (d, sib)).wait_recv()

    def from_y(i, js):
        ys = y_peers[i] // 4
        for j, (src, dst, at) in enumerate(weights(ys, c)):
            if j not in js:
                continue
            remote(src, dst.at[at], w_s.at[0], w_r.at[4 * ys + j], (d, y_peers[i])).wait_recv()
            if i < 2 and j % 2 == i:
                cp = remote(
                    dst.at[at], dst.at[at], w_s.at[8 + j], w_r.at[4 * ys + j], (d, y_peers[1 - i]))
                cp.start()
                waits.append(cp.wait_send)
            cp = remote(dst.at[at], dst.at[at], f_s.at[4 * ys + j], f_r.at[4 * ys + j], (d, sib))
            cp.start()
            waits.append(cp.wait_send)

    def pass_tokens():
        for cp in own_q:
            cp.wait()
        for s in q_peers:
            for p in range(2):
                remote(
                    qt.at[:, pl.ds(0, 256)], xbuf.at[p, feat(s), :],
                    q_s.at[0], q_r.at[q_at(s) + p], (d, s)).wait_recv()
        for k in range(4):
            for p in range(2):
                block = xbuf.at[p, pl.ds(pl.multiple_of(256 * k + 128 * xhi, 128), 128), :]
                cp = remote(block, block, r_s.at[2 * k + p], r_r.at[2 * k + p], (d, flip))
                cp.start()
                waits.append(cp.wait_send)

    z = d // 2
    cross = (wqall, woall)

    def across_send():
        for j, dst in enumerate(cross):
            at = 4 * z + 2 * xhi + c
            cp = remote(dst.at[at], dst.at[at], h_s.at[j], h_r.at[j], across)
            cp.start()
            waits.append(cp.wait_send)

    def to_sibling(zz, j, piece):
        cp = remote(piece, piece, hf_s.at[2 * zz + j], hf_r.at[2 * zz + j], (d, sib))
        cp.start()
        waits.append(cp.wait_send)

    def across_recv():
        for j, dst in enumerate(cross):
            piece = dst.at[4 * z + 2 * (1 - xhi) + c]
            remote(piece, piece, h_s.at[0], h_r.at[j], across).wait_recv()
            for i, g in enumerate(near_peers):
                cp = remote(piece, piece, z_s.at[2 * i + j], z_r.at[2 * z + j], (g, t))
                cp.start()
                waits.append(cp.wait_send)
            to_sibling(z, j, piece)

    def from_z():
        for g in near_peers:
            for j, dst in enumerate(cross):
                piece = dst.at[4 * (g // 2) + 2 * (1 - xhi) + c]
                remote(piece, piece, z_s.at[0], z_r.at[2 * (g // 2) + j], (g, t)).wait_recv()
                to_sibling(g // 2, j, piece)

    def second(f):
        for rows, g, at, half in first_pieces(f):
            remote(
                sbuf.at[f, g, rows], rbuf[f].at[g, rows],
                a_s.at[0], a_r.at[16 * f + 2 * g + half], (g, at)).wait_recv()
        for i, s in enumerate(tp_peers + [t]):
            for b in range(8):
                k = slot[s * 8 + b]
                pbuf[f, s, b // 2, 8 * (b % 2):8 * (b % 2) + 8, :] = rbuf[f][k // 32, k % 32]
            if i < 15:
                cp = remote(pbuf.at[f, s], near.at[f, :, t], b_s.at[15 * f + i], b_r.at[16 * f + t], (d, s))
                cp.start()
                waits.append(cp.wait_send)
        cp = pltpu.make_async_copy(pbuf.at[f, t], near.at[f, :, t], b_l.at[f])
        cp.start()
        local.append(cp)

    def keyval(f):
        for s in tp_peers:
            remote(pbuf.at[f, s], near.at[f, :, s], b_s.at[0], b_r.at[16 * f + s], (d, s)).wait_recv()
        local[f].wait()

        def body(n, carry):
            cols = pl.ds(pl.multiple_of(512 * lax.rem(n, 2), 512), 512)
            full = pl.ds(pl.multiple_of(512 * n, 512), 512)
            wpart = wkvv[n // 2, WIDE * f:WIDE * (f + 1), cols]
            term = dot(near[f].reshape(1024, WIDE), wpart, ((1,), (0,)))
            if f == 0:
                acc[:, full] = term
            else:
                acc[:, full] += term
            return carry
        lax.fori_loop(0, 4, body, 0)

    pass_tokens()
    for f in range(CHUNKS):
        n = 0
        for k, g in enumerate(db_peers):
            pack(f, g, sbuf)
            for rows, to, at, half in first_pieces(f):
                if to is g:
                    cp = remote(
                        sbuf.at[f, g, rows], rbuf[f].at[d, rows],
                        a_s.at[11 * f + n], a_r.at[16 * f + 2 * d + half], (g, at))
                    cp.start()
                    waits.append(cp.wait_send)
                    n += 1
        pack_own(f)

    local = []
    ys = [s // 4 for s in y_peers]
    for cp in own:
        cp.wait()
    from_y(0, (0, 1))
    from_y(1, (0, 1))
    second(0)
    from_y(2, (0, 1))
    across_send()
    from_y(0, (2,))
    from_y(1, (3,))
    tokens()
    feed(mine, True)
    from_sibling(y, (2, 3))
    feed(2 * y + 1 - c, False)
    second(1)
    from_y(0, (3,))
    from_y(1, (2,))
    across_recv()
    feed(2 * ys[0] + c, False)
    feed(2 * ys[1] + c, False)
    second(2)
    for i in range(2):
        from_sibling(ys[i], (2, 3))
        feed(2 * ys[i] + 1 - c, False)
    from_z()
    from_y(2, (2, 3))
    second(3)
    feed(2 * ys[2] + c, False)
    from_sibling(ys[2], (2, 3))
    feed(2 * ys[2] + 1 - c, False)
    psend[...] = part[1 - xhi].astype(BF)
    swap = remote(psend, precv, p_s, p_r, (d, flip))
    swap.start()
    keyval(0)
    keyval(1)
    keyval(2)

    swap.wait()
    enc = (xtok[xhi].astype(F32) + (part[xhi] + precv[...].astype(F32))).astype(BF).astype(F32)
    encoded[...] = enc
    scale = lax.rsqrt(jnp.mean(enc * enc, axis=1, keepdims=True) + 1e-06)
    normed = (enc * scale * gain[...]).astype(BF)
    for k in range(4):
        from_sibling(k, (0, 1))
        for j, (src, dst) in enumerate(((wqt, wqall), (wo, woall))):
            at = 4 * k + 2 * (1 - xhi) + 1 - c
            remote(src, dst.at[at], hf_s.at[0], hf_r.at[2 * k + j], (d, sib)).wait_recv()
    for e in range(4):
        wpart = wqall[4 * e:4 * e + 4].reshape(256, 1024)
        query[:, 256 * e:256 * e + 256] = (dot(normed, wpart, ((1,), (1,))) * 0.125).astype(BF)

    keyval(3)
    lane = lax.broadcasted_iota(jnp.int32, (1, 128), 1)
    low = (lane < 64).astype(F32).astype(BF)
    high = (lane >= 64).astype(F32).astype(BF)
    give = []
    for half in range(2):
        def body(m, carry):
            qrows = pl.ds(pl.multiple_of(64 * m, 64), 64)
            krows = pl.ds(pl.multiple_of(256 * m, 256), 256)
            for pair in range(8):
                cols = slice(128 * pair, 128 * pair + 128)
                vcols = slice(1024 + 128 * pair, 1024 + 128 * pair + 128)
                qp = query[qrows, cols]
                both = jnp.concatenate([qp * low, qp * high], axis=0)
                s = dot(both, acc[krows, cols].astype(BF), ((1,), (1,)))
                e = jnp.exp(s - jnp.max(s, axis=1, keepdims=True))
                total = jnp.sum(e, axis=1, keepdims=True)
                o = dot(e.astype(BF), acc[krows, vcols].astype(BF), ((1,), (0,))) / total
                ctx[qrows, cols] = jnp.where(lane < 64, o[:64], o[64:]).astype(BF)
            return carry
        lax.fori_loop(2 * half, 2 * half + 2, body, 0)
        rows = slice(128 * half, 128 * half + 128)
        for e in range(4):
            cols = slice(256 * e, 256 * e + 256)
            wpart = woall[:, :, cols].reshape(1024, 256)
            m = encoded[rows, cols] + dot(ctx[rows, :], wpart, ((1,), (0,)))
            outt[half, cols, :] = m.T.astype(BF)
        at = pl.ds(pl.multiple_of(256 * t + 128 * half, 128), 128)
        for i, s in enumerate(tp_peers):
            cp = remote(
                outt.at[half, feat(s), :], out.at[:, at],
                g_s.at[15 * half + i], g_r.at[16 * half + t], (d, s))
            cp.start()
            waits.append(cp.wait_send)
        cp = pltpu.make_async_copy(outt.at[half, feat(t), :], out.at[:, at], g_l.at[half])
        cp.start()
        waits.append(cp.wait)
    for half in range(2):
        for s in tp_peers:
            at = pl.ds(pl.multiple_of(256 * s + 128 * half, 128), 128)
            remote(
                outt.at[half, feat(s), :], out.at[:, at],
                g_s.at[0], g_r.at[16 * half + s], (d, s)).wait_recv()
    for w in waits:
        w()


def step(slot, want, gain, qt, up, down, wqt, wo, wkv, base):
    D = pltpu.SemaphoreType.DMA
    V = pltpu.VMEM
    return pl.pallas_call(
        step_kernel,
        name="step",
        out_shape=jax.ShapeDtypeStruct((64, 4096), BF),
        in_specs=[SM, VM, VM, ANY, ANY, ANY, ANY, ANY, ANY, ANY],
        out_specs=ANY,
        scratch_shapes=[
            V((256, 8, 1024), F32),
            V((CHUNKS, 8, 32, 8, WIDE), BF),
            *(V((8, 32, 8, WIDE), BF) for _ in range(CHUNKS)),
            V((CHUNKS, 16, 4, 16, WIDE), BF),
            V((CHUNKS, 4, 16, 16, WIDE), BF),
            V((2, 1024, 256), BF),
            V((2, 256, 1024), BF),
            V((8, 1024, 256), BF),
            V((8, 256, 1024), BF),
            V((16, 64, 1024), BF),
            V((16, 64, 1024), BF),
            V((2, 1024, 1024), BF),
            V((2, 256, 1024), F32),
            V((256, 1024), BF),
            V((256, 1024), BF),
            V((256, 1024), F32),
            V((256, 1024), BF),
            V((1024, 2048), F32),
            V((256, 1024), BF),
            V((2, 1024, 128), BF),
            V((8, 8, 128), jnp.int32),
            pltpu.SMEM((8, 8, 128), jnp.int32),
            D, D((7,)), D((8,)), D((2,)), D((14,)), D((16,)), D((2,)), D((8,)), D((8,)),
            D((12,)), D((16,)), D((5,)), D((16,)), D((16,)),
            D((2,)), D((2,)), D((6,)), D((8,)), D((8,)), D((8,)),
            D((11 * CHUNKS,)), D((16 * CHUNKS,)), D((15 * CHUNKS,)), D((16 * CHUNKS,)), D((CHUNKS,)),
            D, D, D((30,)), D((32,)), D((2,)),
        ],
        compiler_params=pltpu.CompilerParams(
            collective_id=0, has_side_effects=True, vmem_limit_bytes=59 << 20
        ),
    )(slot, want, gain, qt, up, down, wqt, wo, wkv, base)


def per_device(
    queries, enc_up, enc_down, attn_gain, w_query, w_keyval, w_out, database, nb_owner, nb_row
):
    owners = nb_owner.reshape(128)
    rows = nb_row.reshape(128)
    i = jnp.arange(128)
    rank = jnp.sum(
        ((owners[:, None] == owners[None, :]) & (i[None, :] < i[:, None])).astype(jnp.int32), axis=1)
    slot = owners * 32 + rank
    lane = jnp.arange(128)
    key = jnp.where((lane < 32)[None, :], lane[None, :] + 32 * jnp.arange(8)[:, None], -1)
    want = jnp.sum(
        jnp.where(key[:, :, None] == slot[None, None, :], rows[None, None, :], 0), axis=2)
    want = jnp.broadcast_to(want[:, None, :], (8, 8, 128))
    out = step(
        slot, want, attn_gain[None, :], queries.T, enc_up, enc_down, w_query.T, w_out,
        w_keyval, database)
    return out.T


def solution(mesh):
    placed = (
        P("db", "tp"),
        P(None, "tp"),
        P("tp", None),
        P(),
        P(None, "tp"),
        P(),
        P("tp", None),
        P("db", "tp", None),
        P("db", None),
        P("db", None),
    )
    return jax.shard_map(
        per_device, mesh=mesh, in_specs=placed, out_specs=P("db", "tp"), check_vma=False
    )
```
